32 devices in a mesh: groups: 2 (over y), tok: 16 (over z, x, core).
Axes of the slice: x: 2, y: 2, z: 4, core: 2. Of those that a mesh axis runs over, the one named last changes fastest.
Arguments:
- queries: bfloat16 [2048, 2048], P(('groups', 'tok')), parts along dimension 0, may hold values from -256 to 256, as said below
- fresh_keys: bfloat16 [2048, 2048], P(('groups', 'tok')), parts along dimension 0, may hold values from -6 to 6, as said below
- fresh_values: bfloat16 [2048, 2048], P(('groups', 'tok')), parts along dimension 0, may hold values from -6 to 6
- stale_keys: bfloat16 [2048, 2048], P(('groups', 'tok')), parts along dimension 0, may hold values from -6 to 6
- stale_values: bfloat16 [2048, 2048], P(('groups', 'tok')), parts along dimension 0, may hold values from -6 to 6
- patch_starts: int32 [32], P('groups'), parts along dimension 0, may hold values from 0 to 1023, as said below
- order_starts: int32 [32], P('groups'), parts along dimension 0, may hold values from 0 to 1023, as said below
Outputs:
- attended: bfloat16 [2048, 2048], P(('groups', 'tok')), parts along dimension 0
The draws below stay inside these ranges and needn't reach their ends.
There are 2 independent parts, one for each index of `groups`. The reference program is written for one: setup_inputs(seed, part) draws one part's arguments, and reference() takes and returns one part's arrays. A program takes and returns all parts, laid end to end along the dimension named above; each array names one. Nothing has to cross between parts.
Inputs may be any that keep to these rules, and one draw needn't show every extreme that they name: `patch_starts`: strictly increasing; the first entry is 0. `order_starts`: the entries of patch_starts, each once, in processing order. `queries`: entries are finite. `fresh_keys`: entries are finite.
All inputs are finite; a program needn't handle non-finite values.
Results may differ from the reference program's by a relative error of at most 0.0049.
Values may be sent and summed in bfloat16 or wider, within the bound.
A program may use at most 128 MiB of HBM per device.

```python
import math
import jax
import jax.numpy as jnp
from jax import lax

HEADS = 16
HEAD_DIM = 128
PATCHES = 16
TOKENS = 1024


def shared_keys(key):
    draws = jax.random.normal(jax.random.fold_in(key, 11), (TOKENS, HEADS * HEAD_DIM), jnp.float32)
    return jnp.clip(draws, -6.0, 6.0)


def draw_fresh_keys(key, part):
    return shared_keys(key).astype(jnp.bfloat16)


def draw_queries(key, part):
    base_key = jax.random.fold_in(key, 23)
    draws = jax.random.normal(base_key, (TOKENS, HEADS * HEAD_DIM), jnp.float32)
    return (3.0 * jnp.clip(draws, -4.0, 4.0)).astype(jnp.bfloat16)


def patch_layout(key):
    cut_points = jax.random.permutation(jax.random.fold_in(key, 5), TOKENS - 1)[:PATCHES - 1] + 1
    starts = jnp.concatenate([jnp.zeros((1,), jnp.int32), jnp.sort(cut_points.astype(jnp.int32))])
    ordering = jax.random.permutation(jax.random.fold_in(key, 6), PATCHES)
    return (starts, starts[ordering])


def draw_patch_starts(key, part):
    return patch_layout(key)[0].astype(jnp.int32)


def draw_order_starts(key, part):
    return patch_layout(key)[1].astype(jnp.int32)


def levels(key, extent, pieces, low, largest):
    def one(axis_at, parts):
        heights = jax.random.uniform(jax.random.fold_in(jax.random.fold_in(key, 6), axis_at), (parts,), jnp.float32, low / len(pieces), largest / len(pieces))
        return jnp.repeat(jnp.exp(heights), extent[axis_at] // parts).reshape((-1,) + (1,) * (len(extent) - axis_at - 1))

    loudness = one(*pieces[0])
    for cut in pieces[1:]:
        loudness = loudness * one(*cut)
    return loudness


def noise(rng, extent, deviation, reach, shards=(), kind=jnp.bfloat16):
    level = levels(rng, extent, shards, -0.22, 0.18) if shards else 1.0
    drawn = jax.random.normal(rng, extent, jnp.float32) * deviation * level
    return jnp.minimum(jnp.maximum(drawn, -reach), reach).astype(kind)


def setup_inputs(seed: int = 0, part: int = 0) -> dict:
    splits = jax.random.split(jax.random.key(seed), 8)
    part_keys = jax.random.split(jax.random.fold_in(splits[7], part), 8)
    queries = draw_queries(jax.random.fold_in(jax.random.fold_in(splits[7], part), 71), part)
    fresh_keys = draw_fresh_keys(jax.random.fold_in(jax.random.fold_in(splits[7], part), 71), part)
    fresh_values = noise(part_keys[2], (TOKENS, HEADS * HEAD_DIM), 1.0, 6.0, ((0, 16),))
    stale_keys = noise(part_keys[3], (TOKENS, HEADS * HEAD_DIM), 1.0, 6.0, ((0, 16),))
    stale_values = noise(part_keys[4], (TOKENS, HEADS * HEAD_DIM), 1.0, 6.0, ((0, 16),))
    patch_starts = draw_patch_starts(jax.random.fold_in(jax.random.fold_in(splits[7], part), 71), part)
    order_starts = draw_order_starts(jax.random.fold_in(jax.random.fold_in(splits[7], part), 71), part)
    return {"queries": queries, "fresh_keys": fresh_keys, "fresh_values": fresh_values, "stale_keys": stale_keys, "stale_values": stale_values, "patch_starts": patch_starts, "order_starts": order_starts}


def token_ranks(positions, patch_starts, order_starts):
    patch_count = patch_starts.shape[0]
    slot_ids = jnp.arange(patch_count, dtype=jnp.int32)
    patch_of = lax.optimization_barrier(jnp.sum((patch_starts[None, :] <= positions[:, None]).astype(jnp.int32), axis=1)) - 1
    matches = (order_starts[:, None] == patch_starts[None, :]).astype(jnp.int32)
    rank_of = lax.optimization_barrier(jnp.sum(matches * slot_ids[:, None], axis=0))
    one_hot = (patch_of[:, None] == slot_ids[None, :]).astype(jnp.int32)
    return lax.optimization_barrier(jnp.sum(one_hot * rank_of[None, :], axis=1))

def attend_block(query_block, query_rank, key_stack, key_rank):
    dims = (((1,), (1,)), ((), ()))
    score_scale = 1.0 / math.sqrt(query_block.shape[-1])
    fresh_scores = lax.dot_general(query_block, key_stack[0], dims, preferred_element_type=jnp.float32) * score_scale
    stale_scores = lax.dot_general(query_block, key_stack[2], dims, preferred_element_type=jnp.float32) * score_scale
    fresh_ok = key_rank[None, :] <= query_rank[:, None]
    fresh_scores = jnp.where(fresh_ok, fresh_scores, -jnp.inf)
    stale_scores = jnp.where(fresh_ok, -jnp.inf, stale_scores)
    row_max = jnp.maximum(lax.optimization_barrier(jnp.max(fresh_scores, axis=1)), lax.optimization_barrier(jnp.max(stale_scores, axis=1)))[:, None]
    fresh_exp = jnp.exp(fresh_scores - row_max)
    stale_exp = jnp.exp(stale_scores - row_max)
    row_total = lax.optimization_barrier(jnp.sum(fresh_exp, axis=1, keepdims=True)) + lax.optimization_barrier(jnp.sum(stale_exp, axis=1, keepdims=True))
    fresh_probs = (fresh_exp / row_total).astype(jnp.bfloat16)
    stale_probs = (stale_exp / row_total).astype(jnp.bfloat16)
    mixed = jnp.dot(fresh_probs, key_stack[1], preferred_element_type=jnp.float32)
    mixed = mixed + jnp.dot(stale_probs, key_stack[3], preferred_element_type=jnp.float32)
    return mixed.astype(jnp.bfloat16)

def attend_rows(query_rows, query_rank, key_stack, key_rank):
    row_count = query_rows.shape[0]
    block_rows = 512 if row_count % 512 == 0 else row_count
    blocks = row_count // block_rows

    def one_block(inputs):
        return attend_block(inputs[0], inputs[1], key_stack, key_rank)
    result = lax.map(one_block, (query_rows.reshape(blocks, block_rows, query_rows.shape[1]), query_rank.reshape(blocks, block_rows)))
    return result.reshape(row_count, query_rows.shape[1])

def reference(queries, fresh_keys, fresh_values, stale_keys, stale_values, patch_starts, order_starts):
    token_count = queries.shape[0]
    positions = jnp.arange(token_count, dtype=jnp.int32)
    ranks = token_ranks(positions, patch_starts, order_starts)

    def by_head(array):
        return array.reshape(token_count, HEADS, HEAD_DIM).transpose(1, 0, 2)
    stacked = jnp.stack([by_head(fresh_keys), by_head(fresh_values), by_head(stale_keys), by_head(stale_values)], axis=1)

    def one_head(inputs):
        return attend_rows(inputs[0], ranks, inputs[1], ranks)
    attended = lax.map(one_head, (by_head(queries), stacked))
    return attended.transpose(1, 0, 2).reshape(token_count, HEADS * HEAD_DIM)
```

```python
import functools
import math

import jax
import jax.numpy as jnp
from jax import lax
from jax.experimental import pallas as pl
from jax.experimental.pallas import tpu as pltpu
from jax.sharding import PartitionSpec as P

HEADS = 16
HEAD_DIM = 128
MESH = pl.DeviceIdType.MESH


def attention_kernel(
    devices,
    patch_starts,
    order_starts,
    queries,
    fresh_keys,
    stale_keys,
    fresh_values,
    stale_values,
    out_ref,
    q_buf,
    kv_buf,
    p_fresh,
    p_stale,
    o_buf,
    q_rank,
    k_rank,
    send_sems,
    recv_sems,
    own_sem,
    out_send,
    out_recv,
):
    me = lax.axis_index("tok")
    tok_dev = queries.shape[0]
    group_size = devices // HEADS
    slab = tok_dev // group_size
    tokens = devices * tok_dev
    rows = devices * slab
    my_head = me // group_size
    my_member = me % group_size
    barrier = pltpu.get_barrier_semaphore()

    def peer_of(step):
        return lax.rem(me + step, devices)

    def columns(head):
        return pl.ds(pl.multiple_of(head * HEAD_DIM, HEAD_DIM), HEAD_DIM)

    def row_slab(index, size):
        return pl.ds(pl.multiple_of(index * size, size), size)

    def greet(step, carry):
        pl.semaphore_signal(barrier, inc=1, device_id={"tok": peer_of(step)}, device_id_type=MESH)
        return carry

    lax.fori_loop(1, devices, greet, 0)

    sources = (queries, fresh_keys, stale_keys, fresh_values, stale_values)

    def source_view(which, device):
        head, member = device // group_size, device % group_size
        if which == 0:
            return queries.at[row_slab(member, slab), columns(head)]
        return sources[which].at[:, columns(head)]

    def landing(which, device):
        if which == 0:
            return q_buf.at[row_slab(device, slab), :]
        return kv_buf.at[which - 1, row_slab(device, tok_dev), :]

    own = [
        pltpu.make_async_copy(source_view(which, me), landing(which, me), own_sem.at[which])
        for which in range(5)
    ]
    for copy in own:
        copy.start()
    pl.semaphore_wait(barrier, devices - 1)

    for which in range(5):

        def send(step, carry, which=which):
            peer = peer_of(step)
            pltpu.make_async_remote_copy(
                src_ref=source_view(which, peer),
                dst_ref=landing(which, me),
                send_sem=send_sems.at[which],
                recv_sem=recv_sems.at[which],
                device_id={"tok": peer},
                device_id_type=MESH,
            ).start()
            return carry

        lax.fori_loop(1, devices, send, 0)

    patches = patch_starts.shape[0]
    starts = [patch_starts[p] for p in range(patches)]
    orders = [order_starts[p] for p in range(patches)]
    ranks = []
    for p in range(patches):
        rank = jnp.int32(0)
        for i in range(patches):
            rank = rank + jnp.where(orders[i] == starts[p], jnp.int32(i), jnp.int32(0))
        ranks.append(rank)
    jumps = [ranks[0]] + [ranks[p] - ranks[p - 1] for p in range(1, patches)]

    def rank_at(positions):
        total = jnp.zeros(positions.shape, jnp.int32)
        for p in range(patches):
            total = total + jnp.where(positions >= starts[p], jumps[p], 0)
        return total

    k_rank[...] = rank_at(lax.broadcasted_iota(jnp.int32, k_rank.shape, 1))

    def fill_rank(device, carry):
        base = device * tok_dev + my_member * slab
        q_rank[row_slab(device, slab), :] = rank_at(
            base + lax.broadcasted_iota(jnp.int32, (slab, HEAD_DIM), 0)
        )
        return carry

    lax.fori_loop(0, devices, fill_rank, 0)

    def all_of(which):
        size = (devices - 1) * (slab if which == 0 else tok_dev)
        return q_buf.at[0:size, :] if which == 0 else kv_buf.at[which - 1, 0:size, :]

    def arrived(which):
        view = all_of(which)
        pltpu.make_async_copy(view, view, recv_sems.at[which]).wait()
        own[which].wait()

    for which in range(3):
        arrived(which)

    score_scale = 1.0 / math.sqrt(HEAD_DIM)
    block = max(slab, min(rows, (1 << 18) // tokens))
    blocks = rows // block
    dims = (((1,), (1,)), ((), ()))

    def probs_block(i, carry):
        at = row_slab(i, block)
        q = q_buf[at, :]
        fresh = lax.dot_general(q, kv_buf[0], dims, preferred_element_type=jnp.float32)
        stale = lax.dot_general(q, kv_buf[1], dims, preferred_element_type=jnp.float32)
        fresh_ok = k_rank[0:1, :] <= q_rank[at, 0:1]
        scores = jnp.where(fresh_ok, fresh, stale) * score_scale
        top = jnp.max(scores, axis=1, keepdims=True)
        weights = jnp.exp(scores - top)
        total = jnp.sum(weights, axis=1, keepdims=True)
        probs = weights * (1.0 / total)
        p_fresh[at, :] = jnp.where(fresh_ok, probs, 0.0).astype(jnp.bfloat16)
        p_stale[at, :] = jnp.where(fresh_ok, 0.0, probs).astype(jnp.bfloat16)
        return carry

    lax.fori_loop(0, blocks, probs_block, 0)

    for which in range(3, 5):
        arrived(which)

    per_block = block // slab

    def give_back(i):
        def one(j, carry):
            target = i * per_block + j

            @pl.when(target != me)
            def _():
                pltpu.make_async_remote_copy(
                    src_ref=o_buf.at[row_slab(target, slab), :],
                    dst_ref=out_ref.at[row_slab(my_member, slab), columns(my_head)],
                    send_sem=out_send,
                    recv_sem=out_recv,
                    device_id={"tok": target},
                    device_id_type=MESH,
                ).start()

            return carry

        lax.fori_loop(0, per_block, one, 0)

    def attend_block(i, carry):
        at = row_slab(i, block)
        mixed = jnp.dot(p_fresh[at, :], kv_buf[2], preferred_element_type=jnp.float32)
        mixed = mixed + jnp.dot(p_stale[at, :], kv_buf[3], preferred_element_type=jnp.float32)
        o_buf[at, :] = mixed.astype(jnp.bfloat16)
        give_back(i)
        return carry

    lax.fori_loop(0, blocks, attend_block, 0)
    mine = pltpu.make_async_copy(
        o_buf.at[row_slab(me, slab), :],
        out_ref.at[row_slab(my_member, slab), columns(my_head)],
        own_sem.at[0],
    )
    mine.start()
    for which in range(5):
        view = all_of(which)
        pltpu.make_async_copy(view, view, send_sems.at[which]).wait()
    view = o_buf.at[0 : (devices - 1) * slab, :]
    mine.wait()
    pltpu.make_async_copy(view, view, out_send).wait()
    pltpu.make_async_copy(view, view, out_recv).wait()


def shards(queries, fresh_keys, fresh_values, stale_keys, stale_values, patch_starts, order_starts):
    devices = lax.axis_size("tok")
    tok_dev, width = queries.shape
    slab = tok_dev // (devices // HEADS)
    tokens, rows = devices * tok_dev, devices * slab
    anywhere = pl.BlockSpec(memory_space=pl.ANY)
    scalars = pl.BlockSpec(memory_space=pltpu.SMEM)
    return pl.pallas_call(
        functools.partial(attention_kernel, devices),
        out_shape=jax.ShapeDtypeStruct((tok_dev, width), jnp.bfloat16),
        in_specs=[scalars] * 2 + [anywhere] * 5,
        out_specs=pl.BlockSpec(memory_space=pltpu.VMEM),
        scratch_shapes=[
            pltpu.VMEM((rows, HEAD_DIM), jnp.bfloat16),
            pltpu.VMEM((4, tokens, HEAD_DIM), jnp.bfloat16),
            pltpu.VMEM((rows, tokens), jnp.bfloat16),
            pltpu.VMEM((rows, tokens), jnp.bfloat16),
            pltpu.VMEM((rows, HEAD_DIM), jnp.bfloat16),
            pltpu.VMEM((rows, HEAD_DIM), jnp.int32),
            pltpu.VMEM((8, tokens), jnp.int32),
            pltpu.SemaphoreType.DMA((5,)),
            pltpu.SemaphoreType.DMA((5,)),
            pltpu.SemaphoreType.DMA((5,)),
            pltpu.SemaphoreType.DMA,
            pltpu.SemaphoreType.DMA,
        ],
        compiler_params=pltpu.CompilerParams(
            collective_id=0, has_side_effects=True, vmem_limit_bytes=60 * 1024 * 1024
        ),
    )(
        patch_starts,
        order_starts,
        queries,
        fresh_keys,
        stale_keys,
        fresh_values,
        stale_values,
    )


def solution(mesh):
    placed = (P(("groups", "tok"), None),) * 5 + (P("groups"),) * 2
    return jax.shard_map(
        shards, mesh=mesh, in_specs=placed, out_specs=P(("groups", "tok"), None), check_vma=False
    )
```

```python
import functools
import math

import jax
import jax.numpy as jnp
from jax import lax
from jax.experimental import pallas as pl
from jax.experimental.pallas import tpu as pltpu
from jax.sharding import PartitionSpec as P

HEADS = 16
HEAD_DIM = 128
MESH = pl.DeviceIdType.MESH


def attention_kernel(
    devices,
    patch_starts,
    order_starts,
    queries,
    fresh_keys,
    stale_keys,
    fresh_values,
    stale_values,
    out_ref,
    q_buf,
    kv_buf,
    p_fresh,
    p_stale,
    o_buf,
    q_rank,
    k_rank,
    send_sems,
    recv_sems,
    own_sem,
    out_send,
    out_recv,
):
    me = lax.axis_index("tok")
    tok_dev = queries.shape[0]
    group_size = devices // HEADS
    slab = tok_dev // group_size
    tokens = devices * tok_dev
    rows = devices * slab
    my_head = me // group_size
    my_member = me % group_size
    barrier = pltpu.get_barrier_semaphore()

    def peer_of(step):
        return lax.rem(me + step, devices)

    def columns(head):
        return pl.ds(pl.multiple_of(head * HEAD_DIM, HEAD_DIM), HEAD_DIM)

    def row_slab(index, size):
        return pl.ds(pl.multiple_of(index * size, size), size)

    def greet(step, carry):
        pl.semaphore_signal(barrier, inc=1, device_id={"tok": peer_of(step)}, device_id_type=MESH)
        return carry

    lax.fori_loop(1, devices, greet, 0)

    sources = (queries, fresh_keys, stale_keys, fresh_values, stale_values)

    def source_view(which, device):
        head, member = device // group_size, device % group_size
        if which == 0:
            return queries.at[row_slab(member, slab), columns(head)]
        return sources[which].at[:, columns(head)]

    def landing(which, device):
        if which == 0:
            return q_buf.at[row_slab(device, slab), :]
        return kv_buf.at[which - 1, row_slab(device, tok_dev), :]

    own = [
        pltpu.make_async_copy(source_view(which, me), landing(which, me), own_sem.at[which])
        for which in range(5)
    ]
    for copy in own:
        copy.start()
    pl.semaphore_wait(barrier, devices - 1)

    for which in range(5):

        def send(step, carry, which=which):
            peer = peer_of(step)
            pltpu.make_async_remote_copy(
                src_ref=source_view(which, peer),
                dst_ref=landing(which, me),
                send_sem=send_sems.at[which],
                recv_sem=recv_sems.at[which],
                device_id={"tok": peer},
                device_id_type=MESH,
            ).start()
            return carry

        lax.fori_loop(1, devices, send, 0)

    patches = patch_starts.shape[0]
    starts = [patch_starts[p] for p in range(patches)]
    orders = [order_starts[p] for p in range(patches)]
    ranks = []
    for p in range(patches):
        rank = jnp.int32(0)
        for i in range(patches):
            rank = rank + jnp.where(orders[i] == starts[p], jnp.int32(i), jnp.int32(0))
        ranks.append(rank)
    jumps = [ranks[0]] + [ranks[p] - ranks[p - 1] for p in range(1, patches)]

    def rank_at(positions):
        total = jnp.zeros(positions.shape, jnp.int32)
        for p in range(patches):
            total = total + jnp.where(positions >= starts[p], jumps[p], 0)
        return total

    k_rank[...] = rank_at(lax.broadcasted_iota(jnp.int32, k_rank.shape, 1))

    def fill_rank(device, carry):
        base = device * tok_dev + my_member * slab
        q_rank[row_slab(device, slab), :] = rank_at(
            base + lax.broadcasted_iota(jnp.int32, (slab, HEAD_DIM), 0)
        )
        return carry

    lax.fori_loop(0, devices, fill_rank, 0)

    def all_of(which):
        size = (devices - 1) * (slab if which == 0 else tok_dev)
        return q_buf.at[0:size, :] if which == 0 else kv_buf.at[which - 1, 0:size, :]

    def arrived(which):
        view = all_of(which)
        pltpu.make_async_copy(view, view, recv_sems.at[which]).wait()
        own[which].wait()

    for which in range(3):
        arrived(which)

    score_scale = 1.0 / math.sqrt(HEAD_DIM)
    block = max(slab, min(rows, (1 << 18) // tokens))
    blocks = rows // block
    dims = (((1,), (1,)), ((), ()))

    def probs_block(i, carry):
        at = row_slab(i, block)
        q = q_buf[at, :]
        fresh = lax.dot_general(q, kv_buf[0], dims, preferred_element_type=jnp.float32)
        stale = lax.dot_general(q, kv_buf[1], dims, preferred_element_type=jnp.float32)
        fresh_ok = k_rank[0:1, :] <= q_rank[at, 0:1]
        scores = jnp.where(fresh_ok, fresh, stale) * score_scale
        top = jnp.max(scores, axis=1, keepdims=True)
        weights = jnp.exp(scores - top)
        total = jnp.sum(weights, axis=1, keepdims=True)
        probs = weights * (1.0 / total)
        p_fresh[at, :] = jnp.where(fresh_ok, probs, 0.0).astype(jnp.bfloat16)
        p_stale[at, :] = jnp.where(fresh_ok, 0.0, probs).astype(jnp.bfloat16)
        return carry

    lax.fori_loop(0, blocks, probs_block, 0)

    for which in range(3, 5):
        arrived(which)

    per_block = block // slab

    def give_back(i):
        def one(j, carry):
            target = i * per_block + j

            @pl.when(target != me)
            def _():
                pltpu.make_async_remote_copy(
                    src_ref=o_buf.at[row_slab(target, slab), :],
                    dst_ref=out_ref.at[row_slab(my_member, slab), columns(my_head)],
                    send_sem=out_send,
                    recv_sem=out_recv,
                    device_id={"tok": target},
                    device_id_type=MESH,
                ).start()

            return carry

        lax.fori_loop(0, per_block, one, 0)

    def attend_block(i, carry):
        at = row_slab(i, block)
        mixed = jnp.dot(p_fresh[at, :], kv_buf[2], preferred_element_type=jnp.float32)
        mixed = mixed + jnp.dot(p_stale[at, :], kv_buf[3], preferred_element_type=jnp.float32)
        o_buf[at, :] = mixed.astype(jnp.bfloat16)
        give_back(i)
        return carry

    lax.fori_loop(0, blocks, attend_block, 0)
    mine = pltpu.make_async_copy(
        o_buf.at[row_slab(me, slab), :],
        out_ref.at[row_slab(my_member, slab), columns(my_head)],
        own_sem.at[0],
    )
    mine.start()
    for which in range(5):
        view = all_of(which)
        pltpu.make_async_copy(view, view, send_sems.at[which]).wait()
    view = o_buf.at[0 : (devices - 1) * slab, :]
    mine.wait()
    pltpu.make_async_copy(view, view, out_send).wait()
    pltpu.make_async_copy(view, view, out_recv).wait()


def shards(queries, fresh_keys, fresh_values, stale_keys, stale_values, patch_starts, order_starts):
    devices = lax.axis_size("tok")
    tok_dev, width = queries.shape
    slab = tok_dev // (devices // HEADS)
    tokens, rows = devices * tok_dev, devices * slab
    anywhere = pl.BlockSpec(memory_space=pl.ANY)
    scalars = pl.BlockSpec(memory_space=pltpu.SMEM)
    return pl.pallas_call(
        functools.partial(attention_kernel, devices),
        out_shape=jax.ShapeDtypeStruct((tok_dev, width), jnp.bfloat16),
        in_specs=[scalars] * 2 + [anywhere] * 5,
        out_specs=anywhere,
        scratch_shapes=[
            pltpu.VMEM((rows, HEAD_DIM), jnp.bfloat16),
            pltpu.VMEM((4, tokens, HEAD_DIM), jnp.bfloat16),
            pltpu.VMEM((rows, tokens), jnp.bfloat16),
            pltpu.VMEM((rows, tokens), jnp.bfloat16),
            pltpu.VMEM((rows, HEAD_DIM), jnp.bfloat16),
            pltpu.VMEM((rows, HEAD_DIM), jnp.int32),
            pltpu.VMEM((8, tokens), jnp.int32),
            pltpu.SemaphoreType.DMA((5,)),
            pltpu.SemaphoreType.DMA((5,)),
            pltpu.SemaphoreType.DMA((5,)),
            pltpu.SemaphoreType.DMA,
            pltpu.SemaphoreType.DMA,
        ],
        compiler_params=pltpu.CompilerParams(
            collective_id=0, has_side_effects=True, vmem_limit_bytes=60 * 1024 * 1024
        ),
    )(
        patch_starts,
        order_starts,
        queries,
        fresh_keys,
        stale_keys,
        fresh_values,
        stale_values,
    )


def rank_table(patch_starts, order_starts):
    patches = patch_starts.shape[0]
    starts = [patch_starts[p] for p in range(patches)]
    orders = [order_starts[p] for p in range(patches)]
    ranks = []
    for p in range(patches):
        rank = jnp.int32(0)
        for i in range(patches):
            rank = rank + jnp.where(orders[i] == starts[p], jnp.int32(i), jnp.int32(0))
        ranks.append(rank)
    jumps = [ranks[0]] + [ranks[p] - ranks[p - 1] for p in range(1, patches)]

    def rank_at(positions):
        total = jnp.zeros(positions.shape, jnp.int32)
        for p in range(patches):
            total = total + jnp.where(positions >= starts[p], jumps[p], 0)
        return total

    return rank_at


def halves_kernel(
    devices,
    patch_starts,
    order_starts,
    queries,
    fresh_keys,
    stale_keys,
    fresh_values,
    stale_values,
    parts_ref,
    stats_ref,
    q_buf,
    kv_buf,
    p_fresh,
    p_stale,
    o_buf,
    s_buf,
    q_rank,
    k_rank,
    q_send,
    q_recv,
    kv_send,
    kv_recv,
    own_sem,
    own_kv_sem,
    o_send,
    o_recv,
    s_send,
    s_recv,
):
    me = lax.axis_index("tok")
    tok_dev = queries.shape[0]
    half = devices // 2
    held = HEADS // half
    tokens = devices * tok_dev
    keys = half * tok_dev
    side, place = me // half, me % half
    barrier = pltpu.get_barrier_semaphore()

    def peer_of(step):
        return lax.rem(me + step, devices)

    def near_peer(step):
        return side * half + lax.rem(place + step, half)

    def columns(start, count=1):
        return pl.ds(pl.multiple_of(start * HEAD_DIM, HEAD_DIM), count * HEAD_DIM)

    def row_slab(index, size):
        return pl.ds(pl.multiple_of(index * size, size), size)

    def greet(step, carry):
        pl.semaphore_signal(barrier, inc=1, device_id={"tok": peer_of(step)}, device_id_type=MESH)
        return carry

    lax.fori_loop(1, devices, greet, 0)

    sources = (fresh_keys, stale_keys, fresh_values, stale_values)

    def q_source(device):
        return queries.at[:, columns(device % half * held, held)]

    def kv_source(head, which, device):
        return sources[which].at[:, columns(device % half * held + head)]

    def q_landing(device):
        return q_buf.at[row_slab(device, tok_dev), :]

    def kv_landing(head, which, device):
        return kv_buf.at[head, which, row_slab(device % half, tok_dev), :]

    own_q = pltpu.make_async_copy(q_source(me), q_landing(me), own_sem.at[0])
    own_q.start()
    own_kv = [
        [
            pltpu.make_async_copy(
                kv_source(head, which, me), kv_landing(head, which, me), own_kv_sem.at[head, which]
            )
            for which in range(4)
        ]
        for head in range(held)
    ]
    for group in own_kv:
        for copy in group:
            copy.start()
    pl.semaphore_wait(barrier, devices - 1)

    def send_q(step, carry):
        peer = peer_of(step)
        pltpu.make_async_remote_copy(
            src_ref=q_source(peer),
            dst_ref=q_landing(me),
            send_sem=q_send,
            recv_sem=q_recv,
            device_id={"tok": peer},
            device_id_type=MESH,
        ).start()
        return carry

    lax.fori_loop(1, devices, send_q, 0)
    for head in range(held):
        for which in range(4):

            def send_kv(step, carry, head=head, which=which):
                peer = near_peer(step)
                pltpu.make_async_remote_copy(
                    src_ref=kv_source(head, which, peer),
                    dst_ref=kv_landing(head, which, me),
                    send_sem=kv_send.at[head, which],
                    recv_sem=kv_recv.at[head, which],
                    device_id={"tok": peer},
                    device_id_type=MESH,
                ).start()
                return carry

            lax.fori_loop(1, half, send_kv, 0)

    rank_at = rank_table(patch_starts, order_starts)
    k_rank[...] = rank_at(keys * side + lax.broadcasted_iota(jnp.int32, k_rank.shape, 1))

    def fill_rank(device, carry):
        q_rank[row_slab(device, tok_dev), :] = rank_at(
            device * tok_dev + lax.broadcasted_iota(jnp.int32, (tok_dev, HEAD_DIM), 0)
        )
        return carry

    lax.fori_loop(0, devices, fill_rank, 0)

    def whole_wait(view, sem):
        pltpu.make_async_copy(view, view, sem).wait()

    q_all = q_buf.at[0 : (devices - 1) * tok_dev, :]

    def kv_all(head, which):
        return kv_buf.at[head, which, 0 : (half - 1) * tok_dev, :]

    def arrived(head, which):
        whole_wait(kv_all(head, which), kv_recv.at[head, which])
        own_kv[head][which].wait()

    whole_wait(q_all, q_recv)
    own_q.wait()

    score_scale = 1.0 / math.sqrt(HEAD_DIM)
    block = min(tokens, 256)
    blocks = tokens // block
    per_block = block // tok_dev
    dims = (((1,), (1,)), ((), ()))
    first_block = me // per_block + blocks // 2
    owner_tile = 128 // tok_dev

    for head in range(held):
        own_columns = slice(head * HEAD_DIM, (head + 1) * HEAD_DIM)
        arrived(head, 0)
        arrived(head, 1)

        def probs_block(i, carry, head=head, own_columns=own_columns):
            at = row_slab(i, block)
            q = q_buf[at, own_columns]
            fresh = lax.dot_general(q, kv_buf[head, 0], dims, preferred_element_type=jnp.float32)
            stale = lax.dot_general(q, kv_buf[head, 1], dims, preferred_element_type=jnp.float32)
            fresh_ok = k_rank[0:1, :] <= q_rank[at, 0:1]
            scores = jnp.where(fresh_ok, fresh, stale) * score_scale
            top = jnp.max(scores, axis=1, keepdims=True)
            weights = jnp.exp(scores - top)
            total = jnp.sum(weights, axis=1, keepdims=True)
            probs = weights * (1.0 / total)
            p_fresh[at, :] = jnp.where(fresh_ok, probs, 0.0).astype(jnp.bfloat16)
            p_stale[at, :] = jnp.where(fresh_ok, 0.0, probs).astype(jnp.bfloat16)
            level = jnp.broadcast_to(top + jnp.log(total), (block, 128))
            for tile in range(block // 128):
                turned = jnp.transpose(level[tile * 128 : (tile + 1) * 128, :])
                s_buf[i * (block // 128) + tile, head : head + 1, :] = turned[0:1, :]
            return carry

        lax.fori_loop(0, blocks, probs_block, 0)
        arrived(head, 2)
        arrived(head, 3)

        if head == held - 1:

            def send_stats(step, carry):
                peer = peer_of(step)
                pltpu.make_async_remote_copy(
                    src_ref=s_buf.at[peer // owner_tile],
                    dst_ref=stats_ref.at[me],
                    send_sem=s_send,
                    recv_sem=s_recv,
                    device_id={"tok": peer},
                    device_id_type=MESH,
                ).start()
                return carry

        def attend_block(t, carry, head=head):
            i = lax.rem(first_block + t, blocks)
            at = row_slab(i, block)
            mixed = jnp.dot(p_fresh[at, :], kv_buf[head, 2], preferred_element_type=jnp.float32)
            mixed = mixed + jnp.dot(
                p_stale[at, :], kv_buf[head, 3], preferred_element_type=jnp.float32
            )
            o_buf[head, at, :] = mixed.astype(jnp.bfloat16)

            def give_back(j, carry):
                target = i * per_block + j

                @pl.when(target != me)
                def _():
                    pltpu.make_async_remote_copy(
                        src_ref=o_buf.at[head, row_slab(target, tok_dev), :],
                        dst_ref=parts_ref.at[side, :, columns(place * held + head)],
                        send_sem=o_send.at[head],
                        recv_sem=o_recv.at[head],
                        device_id={"tok": target},
                        device_id_type=MESH,
                    ).start()

                return carry

            lax.fori_loop(0, per_block, give_back, 0)
            return carry

        lax.fori_loop(0, blocks, attend_block, 0)
        if head == held - 1:
            lax.fori_loop(1, devices, send_stats, 0)

    mine = [
        pltpu.make_async_copy(
            o_buf.at[head, row_slab(me, tok_dev), :],
            parts_ref.at[side, :, columns(place * held + head)],
            own_sem.at[1 + head],
        )
        for head in range(held)
    ]
    mine.append(
        pltpu.make_async_copy(
            s_buf.at[me // owner_tile], stats_ref.at[me], own_sem.at[1 + held]
        )
    )
    for copy in mine:
        copy.start()
    whole_wait(q_all, q_send)
    for head in range(held):
        for which in range(4):
            whole_wait(kv_all(head, which), kv_send.at[head, which])
    for copy in mine:
        copy.wait()
    s_all = stats_ref.at[0 : devices - 1]
    whole_wait(s_all, s_send)
    whole_wait(s_all, s_recv)
    for head in range(held):
        o_all = o_buf.at[head, 0 : (devices - 1) * tok_dev, :]
        whole_wait(o_all, o_send.at[head])
        whole_wait(o_all, o_recv.at[head])


def merge_kernel(devices, parts, stats, out_ref, shares):
    me = lax.axis_index("tok")
    tok_dev = out_ref.shape[0]
    half = devices // 2
    held = HEADS // half

    def levels(side):
        return jnp.concatenate(
            [
                stats[side * half + head // held, head % held : head % held + 1, :]
                for head in range(HEADS)
            ],
            axis=0,
        )

    low, high = levels(0), levels(1)
    share = jnp.concatenate(
        [
            1.0 / (1.0 + jnp.exp(high - low)),
            1.0 / (1.0 + jnp.exp(low - high)),
            jnp.zeros((128 - 2 * HEADS, 128), jnp.float32),
        ],
        axis=0,
    )
    shares[...] = jnp.transpose(share)
    start = pl.multiple_of(me % (128 // tok_dev) * tok_dev, tok_dev)
    mine = shares[pl.ds(start, tok_dev), :]
    for head in range(HEADS):
        at = slice(head * HEAD_DIM, (head + 1) * HEAD_DIM)
        merged = parts[0, :, at].astype(jnp.float32) * mine[:, head : head + 1]
        merged = merged + parts[1, :, at].astype(jnp.float32) * mine[:, HEADS + head : HEADS + head + 1]
        out_ref[:, at] = merged.astype(jnp.bfloat16)


def halves(queries, fresh_keys, fresh_values, stale_keys, stale_values, patch_starts, order_starts):
    devices = lax.axis_size("tok")
    tok_dev, width = queries.shape
    half = devices // 2
    held = HEADS // half
    tokens, keys = devices * tok_dev, half * tok_dev
    anywhere = pl.BlockSpec(memory_space=pl.ANY)
    scalars = pl.BlockSpec(memory_space=pltpu.SMEM)
    vmem = pl.BlockSpec(memory_space=pltpu.VMEM)
    dma = pltpu.SemaphoreType.DMA
    parts, stats = pl.pallas_call(
        functools.partial(halves_kernel, devices),
        out_shape=(
            jax.ShapeDtypeStruct((2, tok_dev, width), jnp.bfloat16),
            jax.ShapeDtypeStruct((devices, held, 128), jnp.float32),
        ),
        in_specs=[scalars] * 2 + [anywhere] * 5,
        out_specs=(anywhere, anywhere),
        scratch_shapes=[
            pltpu.VMEM((tokens, held * HEAD_DIM), jnp.bfloat16),
            pltpu.VMEM((held, 4, keys, HEAD_DIM), jnp.bfloat16),
            pltpu.VMEM((tokens, keys), jnp.bfloat16),
            pltpu.VMEM((tokens, keys), jnp.bfloat16),
            pltpu.VMEM((held, tokens, HEAD_DIM), jnp.bfloat16),
            pltpu.VMEM((tokens // 128, held, 128), jnp.float32),
            pltpu.VMEM((tokens, HEAD_DIM), jnp.int32),
            pltpu.VMEM((8, keys), jnp.int32),
            dma,
            dma,
            dma((held, 4)),
            dma((held, 4)),
            dma((2 + held,)),
            dma((held, 4)),
            dma((held,)),
            dma((held,)),
            dma,
            dma,
        ],
        compiler_params=pltpu.CompilerParams(
            collective_id=0, has_side_effects=True, vmem_limit_bytes=60 * 1024 * 1024
        ),
    )(patch_starts, order_starts, queries, fresh_keys, stale_keys, fresh_values, stale_values)
    return pl.pallas_call(
        functools.partial(merge_kernel, devices),
        out_shape=jax.ShapeDtypeStruct((tok_dev, width), jnp.bfloat16),
        in_specs=[vmem, vmem],
        out_specs=vmem,
        scratch_shapes=[pltpu.VMEM((128, 128), jnp.float32)],
    )(parts, stats)


def solution(mesh):
    placed = (P(("groups", "tok"), None),) * 5 + (P("groups"),) * 2
    devices = mesh.shape["tok"]

    def body(*arrays):
        tok_dev = arrays[0].shape[0]
        split = devices % 2 == 0 and HEADS % (devices // 2) == 0
        split = split and 128 % tok_dev == 0 and devices * tok_dev % 256 == 0
        return (halves if split else shards)(*arrays)

    return jax.shard_map(
        body, mesh=mesh, in_specs=placed, out_specs=P(("groups", "tok"), None), check_vma=False
    )
```

```python
import functools
import math

import jax
import jax.numpy as jnp
from jax import lax
from jax.experimental import pallas as pl
from jax.experimental.pallas import tpu as pltpu
from jax.sharding import PartitionSpec as P

HEADS = 16
HEAD_DIM = 128
MESH = pl.DeviceIdType.MESH


def attention_kernel(
    devices,
    patch_starts,
    order_starts,
    queries,
    fresh_keys,
    stale_keys,
    fresh_values,
    stale_values,
    out_ref,
    q_buf,
    kv_buf,
    p_fresh,
    p_stale,
    o_buf,
    q_rank,
    k_rank,
    send_sems,
    recv_sems,
    own_sem,
    out_send,
    out_recv,
):
    me = lax.axis_index("tok")
    tok_dev = queries.shape[0]
    group_size = devices // HEADS
    slab = tok_dev // group_size
    tokens = devices * tok_dev
    rows = devices * slab
    my_head = me // group_size
    my_member = me % group_size
    barrier = pltpu.get_barrier_semaphore()

    def peer_of(step):
        return lax.rem(me + step, devices)

    def columns(head):
        return pl.ds(pl.multiple_of(head * HEAD_DIM, HEAD_DIM), HEAD_DIM)

    def row_slab(index, size):
        return pl.ds(pl.multiple_of(index * size, size), size)

    def greet(step, carry):
        pl.semaphore_signal(barrier, inc=1, device_id={"tok": peer_of(step)}, device_id_type=MESH)
        return carry

    lax.fori_loop(1, devices, greet, 0)

    sources = (queries, fresh_keys, stale_keys, fresh_values, stale_values)

    def source_view(which, device):
        head, member = device // group_size, device % group_size
        if which == 0:
            return queries.at[row_slab(member, slab), columns(head)]
        return sources[which].at[:, columns(head)]

    def landing(which, device):
        if which == 0:
            return q_buf.at[row_slab(device, slab), :]
        return kv_buf.at[which - 1, row_slab(device, tok_dev), :]

    own = [
        pltpu.make_async_copy(source_view(which, me), landing(which, me), own_sem.at[which])
        for which in range(5)
    ]
    for copy in own:
        copy.start()
    pl.semaphore_wait(barrier, devices - 1)

    for which in range(5):

        def send(step, carry, which=which):
            peer = peer_of(step)
            pltpu.make_async_remote_copy(
                src_ref=source_view(which, peer),
                dst_ref=landing(which, me),
                send_sem=send_sems.at[which],
                recv_sem=recv_sems.at[which],
                device_id={"tok": peer},
                device_id_type=MESH,
            ).start()
            return carry

        lax.fori_loop(1, devices, send, 0)

    patches = patch_starts.shape[0]
    starts = [patch_starts[p] for p in range(patches)]
    orders = [order_starts[p] for p in range(patches)]
    ranks = []
    for p in range(patches):
        rank = jnp.int32(0)
        for i in range(patches):
            rank = rank + jnp.where(orders[i] == starts[p], jnp.int32(i), jnp.int32(0))
        ranks.append(rank)
    jumps = [ranks[0]] + [ranks[p] - ranks[p - 1] for p in range(1, patches)]

    def rank_at(positions):
        total = jnp.zeros(positions.shape, jnp.int32)
        for p in range(patches):
            total = total + jnp.where(positions >= starts[p], jumps[p], 0)
        return total

    k_rank[...] = rank_at(lax.broadcasted_iota(jnp.int32, k_rank.shape, 1))

    def fill_rank(device, carry):
        base = device * tok_dev + my_member * slab
        q_rank[row_slab(device, slab), :] = rank_at(
            base + lax.broadcasted_iota(jnp.int32, (slab, HEAD_DIM), 0)
        )
        return carry

    lax.fori_loop(0, devices, fill_rank, 0)

    def all_of(which):
        size = (devices - 1) * (slab if which == 0 else tok_dev)
        return q_buf.at[0:size, :] if which == 0 else kv_buf.at[which - 1, 0:size, :]

    def arrived(which):
        view = all_of(which)
        pltpu.make_async_copy(view, view, recv_sems.at[which]).wait()
        own[which].wait()

    for which in range(3):
        arrived(which)

    score_scale = 1.0 / math.sqrt(HEAD_DIM)
    block = max(slab, min(rows, (1 << 18) // tokens))
    blocks = rows // block
    dims = (((1,), (1,)), ((), ()))

    def probs_block(i, carry):
        at = row_slab(i, block)
        q = q_buf[at, :]
        fresh = lax.dot_general(q, kv_buf[0], dims, preferred_element_type=jnp.float32)
        stale = lax.dot_general(q, kv_buf[1], dims, preferred_element_type=jnp.float32)
        fresh_ok = k_rank[0:1, :] <= q_rank[at, 0:1]
        scores = jnp.where(fresh_ok, fresh, stale) * score_scale
        top = jnp.max(scores, axis=1, keepdims=True)
        weights = jnp.exp(scores - top)
        total = jnp.sum(weights, axis=1, keepdims=True)
        probs = weights * (1.0 / total)
        p_fresh[at, :] = jnp.where(fresh_ok, probs, 0.0).astype(jnp.bfloat16)
        p_stale[at, :] = jnp.where(fresh_ok, 0.0, probs).astype(jnp.bfloat16)
        return carry

    lax.fori_loop(0, blocks, probs_block, 0)

    for which in range(3, 5):
        arrived(which)

    per_block = block // slab

    def give_back(i):
        def one(j, carry):
            target = i * per_block + j

            @pl.when(target != me)
            def _():
                pltpu.make_async_remote_copy(
                    src_ref=o_buf.at[row_slab(target, slab), :],
                    dst_ref=out_ref.at[row_slab(my_member, slab), columns(my_head)],
                    send_sem=out_send,
                    recv_sem=out_recv,
                    device_id={"tok": target},
                    device_id_type=MESH,
                ).start()

            return carry

        lax.fori_loop(0, per_block, one, 0)

    def attend_block(i, carry):
        at = row_slab(i, block)
        mixed = jnp.dot(p_fresh[at, :], kv_buf[2], preferred_element_type=jnp.float32)
        mixed = mixed + jnp.dot(p_stale[at, :], kv_buf[3], preferred_element_type=jnp.float32)
        o_buf[at, :] = mixed.astype(jnp.bfloat16)
        give_back(i)
        return carry

    lax.fori_loop(0, blocks, attend_block, 0)
    mine = pltpu.make_async_copy(
        o_buf.at[row_slab(me, slab), :],
        out_ref.at[row_slab(my_member, slab), columns(my_head)],
        own_sem.at[0],
    )
    mine.start()
    for which in range(5):
        view = all_of(which)
        pltpu.make_async_copy(view, view, send_sems.at[which]).wait()
    view = o_buf.at[0 : (devices - 1) * slab, :]
    mine.wait()
    pltpu.make_async_copy(view, view, out_send).wait()
    pltpu.make_async_copy(view, view, out_recv).wait()


def shards(queries, fresh_keys, fresh_values, stale_keys, stale_values, patch_starts, order_starts):
    devices = lax.axis_size("tok")
    tok_dev, width = queries.shape
    slab = tok_dev // (devices // HEADS)
    tokens, rows = devices * tok_dev, devices * slab
    anywhere = pl.BlockSpec(memory_space=pl.ANY)
    scalars = pl.BlockSpec(memory_space=pltpu.SMEM)
    return pl.pallas_call(
        functools.partial(attention_kernel, devices),
        out_shape=jax.ShapeDtypeStruct((tok_dev, width), jnp.bfloat16),
        in_specs=[scalars] * 2 + [anywhere] * 5,
        out_specs=anywhere,
        scratch_shapes=[
            pltpu.VMEM((rows, HEAD_DIM), jnp.bfloat16),
            pltpu.VMEM((4, tokens, HEAD_DIM), jnp.bfloat16),
            pltpu.VMEM((rows, tokens), jnp.bfloat16),
            pltpu.VMEM((rows, tokens), jnp.bfloat16),
            pltpu.VMEM((rows, HEAD_DIM), jnp.bfloat16),
            pltpu.VMEM((rows, HEAD_DIM), jnp.int32),
            pltpu.VMEM((8, tokens), jnp.int32),
            pltpu.SemaphoreType.DMA((5,)),
            pltpu.SemaphoreType.DMA((5,)),
            pltpu.SemaphoreType.DMA((5,)),
            pltpu.SemaphoreType.DMA,
            pltpu.SemaphoreType.DMA,
        ],
        compiler_params=pltpu.CompilerParams(
            collective_id=0, has_side_effects=True, vmem_limit_bytes=60 * 1024 * 1024
        ),
    )(
        patch_starts,
        order_starts,
        queries,
        fresh_keys,
        stale_keys,
        fresh_values,
        stale_values,
    )


def rank_table(patch_starts, order_starts):
    patches = patch_starts.shape[0]
    starts = [patch_starts[p] for p in range(patches)]
    orders = [order_starts[p] for p in range(patches)]
    ranks = []
    for p in range(patches):
        rank = jnp.int32(0)
        for i in range(patches):
            rank = rank + jnp.where(orders[i] == starts[p], jnp.int32(i), jnp.int32(0))
        ranks.append(rank)
    jumps = [ranks[0]] + [ranks[p] - ranks[p - 1] for p in range(1, patches)]

    def rank_at(positions):
        total = jnp.zeros(positions.shape, jnp.int32)
        for p in range(patches):
            total = total + jnp.where(positions >= starts[p], jumps[p], 0)
        return total

    return rank_at


def halves_kernel(
    devices,
    patch_starts,
    order_starts,
    queries,
    fresh_keys,
    stale_keys,
    fresh_values,
    stale_values,
    parts_ref,
    shares_ref,
    q_buf,
    kv_buf,
    p_fresh,
    p_stale,
    o_buf,
    s_buf,
    stats_ref,
    shares,
    q_rank,
    k_rank,
    q_send,
    q_recv,
    kv_send,
    kv_recv,
    own_sem,
    own_kv_sem,
    o_send,
    o_recv,
    s_send,
    s_recv,
):
    me = lax.axis_index("tok")
    tok_dev = queries.shape[0]
    half = devices // 2
    held = HEADS // half
    tokens = devices * tok_dev
    keys = half * tok_dev
    side, place = me // half, me % half
    barrier = pltpu.get_barrier_semaphore()

    def peer_of(step):
        return lax.rem(me + step, devices)

    def near_peer(step):
        return side * half + lax.rem(place + step, half)

    def columns(start, count=1):
        return pl.ds(pl.multiple_of(start * HEAD_DIM, HEAD_DIM), count * HEAD_DIM)

    def row_slab(index, size):
        return pl.ds(pl.multiple_of(index * size, size), size)

    def greet(step, carry):
        pl.semaphore_signal(barrier, inc=1, device_id={"tok": peer_of(step)}, device_id_type=MESH)
        return carry

    lax.fori_loop(1, devices, greet, 0)

    sources = (fresh_keys, stale_keys, fresh_values, stale_values)

    def q_source(device):
        return queries.at[:, columns(device % half * held, held)]

    def kv_source(head, which, device):
        return sources[which].at[:, columns(device % half * held + head)]

    def q_landing(device):
        return q_buf.at[row_slab(device, tok_dev), :]

    def kv_landing(head, which, device):
        return kv_buf.at[head, which, row_slab(device % half, tok_dev), :]

    own_q = pltpu.make_async_copy(q_source(me), q_landing(me), own_sem.at[0])
    own_q.start()
    own_kv = [
        [
            pltpu.make_async_copy(
                kv_source(head, which, me), kv_landing(head, which, me), own_kv_sem.at[head, which]
            )
            for which in range(4)
        ]
        for head in range(held)
    ]
    for group in own_kv:
        for copy in group:
            copy.start()
    pl.semaphore_wait(barrier, devices - 1)

    def send_q(step, carry):
        peer = peer_of(step)
        pltpu.make_async_remote_copy(
            src_ref=q_source(peer),
            dst_ref=q_landing(me),
            send_sem=q_send,
            recv_sem=q_recv,
            device_id={"tok": peer},
            device_id_type=MESH,
        ).start()
        return carry

    lax.fori_loop(1, devices, send_q, 0)
    for head in range(held):
        for which in range(4):

            def send_kv(step, carry, head=head, which=which):
                peer = near_peer(step)
                pltpu.make_async_remote_copy(
                    src_ref=kv_source(head, which, peer),
                    dst_ref=kv_landing(head, which, me),
                    send_sem=kv_send.at[head, which],
                    recv_sem=kv_recv.at[head, which],
                    device_id={"tok": peer},
                    device_id_type=MESH,
                ).start()
                return carry

            lax.fori_loop(1, half, send_kv, 0)

    rank_at = rank_table(patch_starts, order_starts)
    k_rank[...] = rank_at(keys * side + lax.broadcasted_iota(jnp.int32, k_rank.shape, 1))

    def fill_rank(device, carry):
        q_rank[row_slab(device, tok_dev), :] = rank_at(
            device * tok_dev + lax.broadcasted_iota(jnp.int32, (tok_dev, HEAD_DIM), 0)
        )
        return carry

    lax.fori_loop(0, devices, fill_rank, 0)

    def whole_wait(view, sem):
        pltpu.make_async_copy(view, view, sem).wait()

    q_all = q_buf.at[0 : (devices - 1) * tok_dev, :]

    def kv_all(head, which):
        return kv_buf.at[head, which, 0 : (half - 1) * tok_dev, :]

    def arrived(head, which):
        whole_wait(kv_all(head, which), kv_recv.at[head, which])
        own_kv[head][which].wait()

    whole_wait(q_all, q_recv)
    own_q.wait()

    score_scale = 1.0 / math.sqrt(HEAD_DIM)
    block = min(tokens, 256)
    blocks = tokens // block
    per_block = block // tok_dev
    dims = (((1,), (1,)), ((), ()))
    first_block = me // per_block + blocks // 2
    owner_tile = 128 // tok_dev

    for head in range(held):
        own_columns = slice(head * HEAD_DIM, (head + 1) * HEAD_DIM)
        arrived(head, 0)
        arrived(head, 1)

        def probs_block(i, carry, head=head, own_columns=own_columns):
            at = row_slab(i, block)
            q = q_buf[at, own_columns]
            fresh = lax.dot_general(q, kv_buf[head, 0], dims, preferred_element_type=jnp.float32)
            stale = lax.dot_general(q, kv_buf[head, 1], dims, preferred_element_type=jnp.float32)
            fresh_ok = k_rank[0:1, :] <= q_rank[at, 0:1]
            scores = jnp.where(fresh_ok, fresh, stale) * score_scale
            top = jnp.max(scores, axis=1, keepdims=True)
            weights = jnp.exp(scores - top)
            total = jnp.sum(weights, axis=1, keepdims=True)
            probs = weights * (1.0 / total)
            p_fresh[at, :] = jnp.where(fresh_ok, probs, 0.0).astype(jnp.bfloat16)
            p_stale[at, :] = jnp.where(fresh_ok, 0.0, probs).astype(jnp.bfloat16)
            level = jnp.broadcast_to(top + jnp.log(total), (block, 128))
            for tile in range(block // 128):
                turned = jnp.transpose(level[tile * 128 : (tile + 1) * 128, :])
                s_buf[i * (block // 128) + tile, head : head + 1, :] = turned[0:1, :]
            return carry

        lax.fori_loop(0, blocks, probs_block, 0)
        arrived(head, 2)
        arrived(head, 3)

        if head == held - 1:

            def send_stats(step, carry):
                peer = peer_of(step)
                pltpu.make_async_remote_copy(
                    src_ref=s_buf.at[peer // owner_tile],
                    dst_ref=stats_ref.at[me],
                    send_sem=s_send,
                    recv_sem=s_recv,
                    device_id={"tok": peer},
                    device_id_type=MESH,
                ).start()
                return carry

        def attend_block(t, carry, head=head):
            i = lax.rem(first_block + t, blocks)
            at = row_slab(i, block)
            mixed = jnp.dot(p_fresh[at, :], kv_buf[head, 2], preferred_element_type=jnp.float32)
            mixed = mixed + jnp.dot(
                p_stale[at, :], kv_buf[head, 3], preferred_element_type=jnp.float32
            )
            o_buf[head, at, :] = mixed.astype(jnp.bfloat16)

            def give_back(j, carry):
                target = i * per_block + j

                @pl.when(target != me)
                def _():
                    pltpu.make_async_remote_copy(
                        src_ref=o_buf.at[head, row_slab(target, tok_dev), :],
                        dst_ref=parts_ref.at[side, :, columns(place * held + head)],
                        send_sem=o_send.at[head],
                        recv_sem=o_recv.at[head],
                        device_id={"tok": target},
                        device_id_type=MESH,
                    ).start()

                return carry

            lax.fori_loop(0, per_block, give_back, 0)
            return carry

        if head == held - 1:
            lax.fori_loop(1, devices, send_stats, 0)
        lax.fori_loop(0, blocks, attend_block, 0)

    mine = [
        pltpu.make_async_copy(
            o_buf.at[head, row_slab(me, tok_dev), :],
            parts_ref.at[side, :, columns(place * held + head)],
            own_sem.at[1 + head],
        )
        for head in range(held)
    ]
    mine.append(
        pltpu.make_async_copy(
            s_buf.at[me // owner_tile], stats_ref.at[me], own_sem.at[1 + held]
        )
    )
    for copy in mine:
        copy.start()
    s_all = stats_ref.at[0 : devices - 1]
    whole_wait(s_all, s_recv)
    mine[-1].wait()

    def levels(of_side):
        return jnp.concatenate(
            [
                stats_ref[of_side * half + head // held, head % held : head % held + 1, :]
                for head in range(HEADS)
            ],
            axis=0,
        )

    low, high = levels(0), levels(1)
    share = jnp.concatenate(
        [
            1.0 / (1.0 + jnp.exp(high - low)),
            1.0 / (1.0 + jnp.exp(low - high)),
            jnp.zeros((128 - 2 * HEADS, 128), jnp.float32),
        ],
        axis=0,
    )
    shares[...] = jnp.transpose(share)
    whole_wait(q_all, q_send)
    for head in range(held):
        for which in range(4):
            whole_wait(kv_all(head, which), kv_send.at[head, which])
    for copy in mine[:-1]:
        copy.wait()
    whole_wait(s_all, s_send)
    put_shares = pltpu.make_async_copy(
        shares.at[row_slab(me % owner_tile, tok_dev), :], shares_ref, own_sem.at[0]
    )
    put_shares.start()
    for head in range(held):
        o_all = o_buf.at[head, 0 : (devices - 1) * tok_dev, :]
        whole_wait(o_all, o_send.at[head])
        whole_wait(o_all, o_recv.at[head])
    put_shares.wait()


def merge_kernel(parts_in, shares_in, out_ref, parts, mine, merged, sems, out_sems):
    width = out_ref.shape[1]
    chunks = out_sems.shape[0]
    wide = width // chunks
    spans = [pl.ds(chunk * wide, wide) for chunk in range(chunks)]
    shares_copy = pltpu.make_async_copy(shares_in, mine, sems.at[chunks])
    shares_copy.start()
    copies = [
        pltpu.make_async_copy(parts_in.at[:, :, at], parts.at[:, :, at], sems.at[chunk])
        for chunk, at in enumerate(spans)
    ]
    for copy in copies:
        copy.start()
    shares_copy.wait()
    outs = []
    for chunk, span in enumerate(spans):
        copies[chunk].wait()
        for head in range(chunk * wide // HEAD_DIM, (chunk + 1) * wide // HEAD_DIM):
            at = slice(head * HEAD_DIM, (head + 1) * HEAD_DIM)
            low = parts[0, :, at].astype(jnp.float32) * mine[:, head : head + 1]
            high = parts[1, :, at].astype(jnp.float32) * mine[:, HEADS + head : HEADS + head + 1]
            merged[:, at] = (low + high).astype(jnp.bfloat16)
        out = pltpu.make_async_copy(merged.at[:, span], out_ref.at[:, span], out_sems.at[chunk])
        out.start()
        outs.append(out)
    for out in outs:
        out.wait()


def halves(queries, fresh_keys, fresh_values, stale_keys, stale_values, patch_starts, order_starts):
    devices = lax.axis_size("tok")
    tok_dev, width = queries.shape
    half = devices // 2
    held = HEADS // half
    tokens, keys = devices * tok_dev, half * tok_dev
    anywhere = pl.BlockSpec(memory_space=pl.ANY)
    scalars = pl.BlockSpec(memory_space=pltpu.SMEM)
    dma = pltpu.SemaphoreType.DMA
    parts, shares = pl.pallas_call(
        functools.partial(halves_kernel, devices),
        out_shape=(
            jax.ShapeDtypeStruct((2, tok_dev, width), jnp.bfloat16),
            jax.ShapeDtypeStruct((tok_dev, 128), jnp.float32),
        ),
        in_specs=[scalars] * 2 + [anywhere] * 5,
        out_specs=(anywhere, anywhere),
        scratch_shapes=[
            pltpu.VMEM((tokens, held * HEAD_DIM), jnp.bfloat16),
            pltpu.VMEM((held, 4, keys, HEAD_DIM), jnp.bfloat16),
            pltpu.VMEM((tokens, keys), jnp.bfloat16),
            pltpu.VMEM((tokens, keys), jnp.bfloat16),
            pltpu.VMEM((held, tokens, HEAD_DIM), jnp.bfloat16),
            pltpu.VMEM((tokens // 128, held, 128), jnp.float32),
            pltpu.VMEM((devices, held, 128), jnp.float32),
            pltpu.VMEM((128, 128), jnp.float32),
            pltpu.VMEM((tokens, HEAD_DIM), jnp.int32),
            pltpu.VMEM((8, keys), jnp.int32),
            dma,
            dma,
            dma((held, 4)),
            dma((held, 4)),
            dma((2 + held,)),
            dma((held, 4)),
            dma((held,)),
            dma((held,)),
            dma,
            dma,
        ],
        compiler_params=pltpu.CompilerParams(
            collective_id=0, has_side_effects=True, vmem_limit_bytes=60 * 1024 * 1024
        ),
    )(patch_starts, order_starts, queries, fresh_keys, stale_keys, fresh_values, stale_values)
    return pl.pallas_call(
        merge_kernel,
        out_shape=jax.ShapeDtypeStruct((tok_dev, width), jnp.bfloat16),
        in_specs=[anywhere, anywhere],
        out_specs=anywhere,
        scratch_shapes=[
            pltpu.VMEM((2, tok_dev, width), jnp.bfloat16),
            pltpu.VMEM((tok_dev, 128), jnp.float32),
            pltpu.VMEM((tok_dev, width), jnp.bfloat16),
            dma((5,)),
            dma((4,)),
        ],
        compiler_params=pltpu.CompilerParams(vmem_limit_bytes=60 * 1024 * 1024),
    )(parts, shares)


def solution(mesh):
    placed = (P(("groups", "tok"), None),) * 5 + (P("groups"),) * 2
    devices = mesh.shape["tok"]

    def body(*arrays):
        tok_dev = arrays[0].shape[0]
        split = devices % 2 == 0 and HEADS % (devices // 2) == 0
        split = split and 128 % tok_dev == 0 and devices * tok_dev % 256 == 0
        return (halves if split else shards)(*arrays)

    return jax.shard_map(
        body, mesh=mesh, in_specs=placed, out_specs=P(("groups", "tok"), None), check_vma=False
    )
```

```python
import functools
import math

import jax
import jax.numpy as jnp
from jax import lax
from jax.experimental import pallas as pl
from jax.experimental.pallas import tpu as pltpu
from jax.sharding import PartitionSpec as P

HEADS = 16
HEAD_DIM = 128
MESH = pl.DeviceIdType.MESH


def attention_kernel(
    devices,
    patch_starts,
    order_starts,
    queries,
    fresh_keys,
    stale_keys,
    fresh_values,
    stale_values,
    out_ref,
    q_buf,
    kv_buf,
    p_fresh,
    p_stale,
    o_buf,
    q_rank,
    k_rank,
    send_sems,
    recv_sems,
    own_sem,
    out_send,
    out_recv,
):
    me = lax.axis_index("tok")
    tok_dev = queries.shape[0]
    group_size = devices // HEADS
    slab = tok_dev // group_size
    tokens = devices * tok_dev
    rows = devices * slab
    my_head = me // group_size
    my_member = me % group_size
    barrier = pltpu.get_barrier_semaphore()

    def peer_of(step):
        return lax.rem(me + step, devices)

    def columns(head):
        return pl.ds(pl.multiple_of(head * HEAD_DIM, HEAD_DIM), HEAD_DIM)

    def row_slab(index, size):
        return pl.ds(pl.multiple_of(index * size, size), size)

    def greet(step, carry):
        pl.semaphore_signal(barrier, inc=1, device_id={"tok": peer_of(step)}, device_id_type=MESH)
        return carry

    lax.fori_loop(1, devices, greet, 0)

    sources = (queries, fresh_keys, stale_keys, fresh_values, stale_values)

    def source_view(which, device):
        head, member = device // group_size, device % group_size
        if which == 0:
            return queries.at[row_slab(member, slab), columns(head)]
        return sources[which].at[:, columns(head)]

    def landing(which, device):
        if which == 0:
            return q_buf.at[row_slab(device, slab), :]
        return kv_buf.at[which - 1, row_slab(device, tok_dev), :]

    own = [
        pltpu.make_async_copy(source_view(which, me), landing(which, me), own_sem.at[which])
        for which in range(5)
    ]
    for copy in own:
        copy.start()
    pl.semaphore_wait(barrier, devices - 1)

    for which in range(5):

        def send(step, carry, which=which):
            peer = peer_of(step)
            pltpu.make_async_remote_copy(
                src_ref=source_view(which, peer),
                dst_ref=landing(which, me),
                send_sem=send_sems.at[which],
                recv_sem=recv_sems.at[which],
                device_id={"tok": peer},
                device_id_type=MESH,
            ).start()
            return carry

        lax.fori_loop(1, devices, send, 0)

    patches = patch_starts.shape[0]
    starts = [patch_starts[p] for p in range(patches)]
    orders = [order_starts[p] for p in range(patches)]
    ranks = []
    for p in range(patches):
        rank = jnp.int32(0)
        for i in range(patches):
            rank = rank + jnp.where(orders[i] == starts[p], jnp.int32(i), jnp.int32(0))
        ranks.append(rank)
    jumps = [ranks[0]] + [ranks[p] - ranks[p - 1] for p in range(1, patches)]

    def rank_at(positions):
        total = jnp.zeros(positions.shape, jnp.int32)
        for p in range(patches):
            total = total + jnp.where(positions >= starts[p], jumps[p], 0)
        return total

    k_rank[...] = rank_at(lax.broadcasted_iota(jnp.int32, k_rank.shape, 1))

    def fill_rank(device, carry):
        base = device * tok_dev + my_member * slab
        q_rank[row_slab(device, slab), :] = rank_at(
            base + lax.broadcasted_iota(jnp.int32, (slab, HEAD_DIM), 0)
        )
        return carry

    lax.fori_loop(0, devices, fill_rank, 0)

    def all_of(which):
        size = (devices - 1) * (slab if which == 0 else tok_dev)
        return q_buf.at[0:size, :] if which == 0 else kv_buf.at[which - 1, 0:size, :]

    def arrived(which):
        view = all_of(which)
        pltpu.make_async_copy(view, view, recv_sems.at[which]).wait()
        own[which].wait()

    for which in range(3):
        arrived(which)

    score_scale = 1.0 / math.sqrt(HEAD_DIM)
    block = max(slab, min(rows, (1 << 18) // tokens))
    blocks = rows // block
    dims = (((1,), (1,)), ((), ()))

    def probs_block(i, carry):
        at = row_slab(i, block)
        q = q_buf[at, :]
        fresh = lax.dot_general(q, kv_buf[0], dims, preferred_element_type=jnp.float32)
        stale = lax.dot_general(q, kv_buf[1], dims, preferred_element_type=jnp.float32)
        fresh_ok = k_rank[0:1, :] <= q_rank[at, 0:1]
        scores = jnp.where(fresh_ok, fresh, stale) * score_scale
        top = jnp.max(scores, axis=1, keepdims=True)
        weights = jnp.exp(scores - top)
        total = jnp.sum(weights, axis=1, keepdims=True)
        probs = weights * (1.0 / total)
        p_fresh[at, :] = jnp.where(fresh_ok, probs, 0.0).astype(jnp.bfloat16)
        p_stale[at, :] = jnp.where(fresh_ok, 0.0, probs).astype(jnp.bfloat16)
        return carry

    lax.fori_loop(0, blocks, probs_block, 0)

    for which in range(3, 5):
        arrived(which)

    per_block = block // slab

    def give_back(i):
        def one(j, carry):
            target = i * per_block + j

            @pl.when(target != me)
            def _():
                pltpu.make_async_remote_copy(
                    src_ref=o_buf.at[row_slab(target, slab), :],
                    dst_ref=out_ref.at[row_slab(my_member, slab), columns(my_head)],
                    send_sem=out_send,
                    recv_sem=out_recv,
                    device_id={"tok": target},
                    device_id_type=MESH,
                ).start()

            return carry

        lax.fori_loop(0, per_block, one, 0)

    def attend_block(i, carry):
        at = row_slab(i, block)
        mixed = jnp.dot(p_fresh[at, :], kv_buf[2], preferred_element_type=jnp.float32)
        mixed = mixed + jnp.dot(p_stale[at, :], kv_buf[3], preferred_element_type=jnp.float32)
        o_buf[at, :] = mixed.astype(jnp.bfloat16)
        give_back(i)
        return carry

    lax.fori_loop(0, blocks, attend_block, 0)
    mine = pltpu.make_async_copy(
        o_buf.at[row_slab(me, slab), :],
        out_ref.at[row_slab(my_member, slab), columns(my_head)],
        own_sem.at[0],
    )
    mine.start()
    for which in range(5):
        view = all_of(which)
        pltpu.make_async_copy(view, view, send_sems.at[which]).wait()
    view = o_buf.at[0 : (devices - 1) * slab, :]
    mine.wait()
    pltpu.make_async_copy(view, view, out_send).wait()
    pltpu.make_async_copy(view, view, out_recv).wait()


def shards(queries, fresh_keys, fresh_values, stale_keys, stale_values, patch_starts, order_starts):
    devices = lax.axis_size("tok")
    tok_dev, width = queries.shape
    slab = tok_dev // (devices // HEADS)
    tokens, rows = devices * tok_dev, devices * slab
    anywhere = pl.BlockSpec(memory_space=pl.ANY)
    scalars = pl.BlockSpec(memory_space=pltpu.SMEM)
    return pl.pallas_call(
        functools.partial(attention_kernel, devices),
        out_shape=jax.ShapeDtypeStruct((tok_dev, width), jnp.bfloat16),
        in_specs=[scalars] * 2 + [anywhere] * 5,
        out_specs=anywhere,
        scratch_shapes=[
            pltpu.VMEM((rows, HEAD_DIM), jnp.bfloat16),
            pltpu.VMEM((4, tokens, HEAD_DIM), jnp.bfloat16),
            pltpu.VMEM((rows, tokens), jnp.bfloat16),
            pltpu.VMEM((rows, tokens), jnp.bfloat16),
            pltpu.VMEM((rows, HEAD_DIM), jnp.bfloat16),
            pltpu.VMEM((rows, HEAD_DIM), jnp.int32),
            pltpu.VMEM((8, tokens), jnp.int32),
            pltpu.SemaphoreType.DMA((5,)),
            pltpu.SemaphoreType.DMA((5,)),
            pltpu.SemaphoreType.DMA((5,)),
            pltpu.SemaphoreType.DMA,
            pltpu.SemaphoreType.DMA,
        ],
        compiler_params=pltpu.CompilerParams(
            collective_id=0, has_side_effects=True, vmem_limit_bytes=60 * 1024 * 1024
        ),
    )(
        patch_starts,
        order_starts,
        queries,
        fresh_keys,
        stale_keys,
        fresh_values,
        stale_values,
    )


def rank_table(patch_starts, order_starts):
    patches = patch_starts.shape[0]
    starts = [patch_starts[p] for p in range(patches)]
    orders = [order_starts[p] for p in range(patches)]
    ranks = []
    for p in range(patches):
        rank = jnp.int32(0)
        for i in range(patches):
            rank = rank + jnp.where(orders[i] == starts[p], jnp.int32(i), jnp.int32(0))
        ranks.append(rank)
    jumps = [ranks[0]] + [ranks[p] - ranks[p - 1] for p in range(1, patches)]

    def rank_at(positions):
        total = jnp.zeros(positions.shape, jnp.int32)
        for p in range(patches):
            total = total + jnp.where(positions >= starts[p], jumps[p], 0)
        return total

    return rank_at


def halves_kernel(
    devices,
    patch_starts,
    order_starts,
    queries,
    fresh_keys,
    stale_keys,
    fresh_values,
    stale_values,
    parts_ref,
    shares_ref,
    q_buf,
    kv_buf,
    p_fresh,
    p_stale,
    o_buf,
    s_buf,
    stats_ref,
    shares,
    q_rank,
    k_rank,
    q_send,
    q_recv,
    kv_send,
    kv_recv,
    own_q_sem,
    own_sem,
    own_kv_sem,
    o_send,
    o_recv,
    s_send,
    s_recv,
):
    me = lax.axis_index("tok")
    tok_dev = queries.shape[0]
    half = devices // 2
    held = HEADS // half
    tokens = devices * tok_dev
    keys = half * tok_dev
    side, place = me // half, me % half
    barrier = pltpu.get_barrier_semaphore()

    def peer_of(step):
        return lax.rem(me + step, devices)

    def near_peer(step):
        return side * half + lax.rem(place + step, half)

    def columns(head):
        return pl.ds(pl.multiple_of(head * HEAD_DIM, HEAD_DIM), HEAD_DIM)

    def row_slab(index, size):
        return pl.ds(pl.multiple_of(index * size, size), size)

    def greet(step, carry):
        pl.semaphore_signal(barrier, inc=1, device_id={"tok": peer_of(step)}, device_id_type=MESH)
        return carry

    lax.fori_loop(1, devices, greet, 0)

    sources = (fresh_keys, stale_keys, fresh_values, stale_values)

    def q_source(head, device):
        return queries.at[:, columns(device % half * held + head)]

    def kv_source(head, which, device):
        return sources[which].at[:, columns(device % half * held + head)]

    def q_landing(head, device):
        return q_buf.at[head, row_slab(device, tok_dev), :]

    def kv_landing(head, which, device):
        return kv_buf.at[head, which, row_slab(device % half, tok_dev), :]

    own_q = [
        pltpu.make_async_copy(q_source(head, me), q_landing(head, me), own_q_sem.at[head])
        for head in range(held)
    ]
    for copy in own_q:
        copy.start()
    own_kv = [
        [
            pltpu.make_async_copy(
                kv_source(head, which, me), kv_landing(head, which, me), own_kv_sem.at[head, which]
            )
            for which in range(4)
        ]
        for head in range(held)
    ]
    for group in own_kv:
        for copy in group:
            copy.start()
    pl.semaphore_wait(barrier, devices - 1)

    for head in range(held):

        def send_q(step, carry, head=head):
            peer = peer_of(step)
            pltpu.make_async_remote_copy(
                src_ref=q_source(head, peer),
                dst_ref=q_landing(head, me),
                send_sem=q_send.at[head],
                recv_sem=q_recv.at[head],
                device_id={"tok": peer},
                device_id_type=MESH,
            ).start()
            return carry

        lax.fori_loop(1, devices, send_q, 0)
        for which in range(4):

            def send_kv(step, carry, head=head, which=which):
                peer = near_peer(step)
                pltpu.make_async_remote_copy(
                    src_ref=kv_source(head, which, peer),
                    dst_ref=kv_landing(head, which, me),
                    send_sem=kv_send.at[head, which],
                    recv_sem=kv_recv.at[head, which],
                    device_id={"tok": peer},
                    device_id_type=MESH,
                ).start()
                return carry

            lax.fori_loop(1, half, send_kv, 0)

    rank_at = rank_table(patch_starts, order_starts)
    k_rank[...] = rank_at(keys * side + lax.broadcasted_iota(jnp.int32, k_rank.shape, 1))

    def fill_rank(device, carry):
        q_rank[row_slab(device, tok_dev), :] = rank_at(
            device * tok_dev + lax.broadcasted_iota(jnp.int32, (tok_dev, HEAD_DIM), 0)
        )
        return carry

    lax.fori_loop(0, devices, fill_rank, 0)

    def whole_wait(view, sem):
        pltpu.make_async_copy(view, view, sem).wait()

    def q_all(head):
        return q_buf.at[head, 0 : (devices - 1) * tok_dev, :]

    def kv_all(head, which):
        return kv_buf.at[head, which, 0 : (half - 1) * tok_dev, :]

    def arrived(head, which):
        whole_wait(kv_all(head, which), kv_recv.at[head, which])
        own_kv[head][which].wait()

    score_scale = 1.0 / math.sqrt(HEAD_DIM)
    block = min(tokens, 512)
    blocks = tokens // block
    per_block = block // tok_dev
    dims = (((1,), (1,)), ((), ()))
    first_block = me // per_block + blocks // 2
    owner_tile = 128 // tok_dev

    for head in range(held):
        whole_wait(q_all(head), q_recv.at[head])
        own_q[head].wait()
        arrived(head, 0)
        arrived(head, 1)

        def probs_block(i, carry, head=head):
            at = row_slab(i, block)
            q = q_buf[head, at, :]
            fresh = lax.dot_general(q, kv_buf[head, 0], dims, preferred_element_type=jnp.float32)
            stale = lax.dot_general(q, kv_buf[head, 1], dims, preferred_element_type=jnp.float32)
            fresh_ok = k_rank[0:1, :] <= q_rank[at, 0:1]
            scores = jnp.where(fresh_ok, fresh, stale) * score_scale
            top = jnp.max(scores, axis=1, keepdims=True)
            weights = jnp.exp(scores - top)
            total = jnp.sum(weights, axis=1, keepdims=True)
            probs = weights * (1.0 / total)
            p_fresh[at, :] = jnp.where(fresh_ok, probs, 0.0).astype(jnp.bfloat16)
            p_stale[at, :] = jnp.where(fresh_ok, 0.0, probs).astype(jnp.bfloat16)
            level = jnp.broadcast_to(top + jnp.log(total), (block, 128))
            for tile in range(block // 128):
                turned = jnp.transpose(level[tile * 128 : (tile + 1) * 128, :])
                s_buf[i * (block // 128) + tile, head : head + 1, :] = turned[0:1, :]
            return carry

        lax.fori_loop(0, blocks, probs_block, 0)
        arrived(head, 2)
        arrived(head, 3)

        if head == held - 1:

            def send_stats(step, carry):
                peer = peer_of(step)
                pltpu.make_async_remote_copy(
                    src_ref=s_buf.at[peer // owner_tile],
                    dst_ref=stats_ref.at[me],
                    send_sem=s_send,
                    recv_sem=s_recv,
                    device_id={"tok": peer},
                    device_id_type=MESH,
                ).start()
                return carry

        def attend_block(t, carry, head=head):
            i = lax.rem(first_block + t, blocks)
            at = row_slab(i, block)
            mixed = jnp.dot(p_fresh[at, :], kv_buf[head, 2], preferred_element_type=jnp.float32)
            mixed = mixed + jnp.dot(
                p_stale[at, :], kv_buf[head, 3], preferred_element_type=jnp.float32
            )
            o_buf[head, at, :] = mixed.astype(jnp.bfloat16)

            def give_back(j, carry):
                target = i * per_block + j

                @pl.when(target != me)
                def _():
                    pltpu.make_async_remote_copy(
                        src_ref=o_buf.at[head, row_slab(target, tok_dev), :],
                        dst_ref=parts_ref.at[side, :, columns(place * held + head)],
                        send_sem=o_send.at[head],
                        recv_sem=o_recv.at[head],
                        device_id={"tok": target},
                        device_id_type=MESH,
                    ).start()

                return carry

            lax.fori_loop(0, per_block, give_back, 0)
            return carry

        if head == held - 1:
            lax.fori_loop(1, devices, send_stats, 0)
        lax.fori_loop(0, blocks, attend_block, 0)

    mine = [
        pltpu.make_async_copy(
            o_buf.at[head, row_slab(me, tok_dev), :],
            parts_ref.at[side, :, columns(place * held + head)],
            own_sem.at[1 + head],
        )
        for head in range(held)
    ]
    mine.append(
        pltpu.make_async_copy(
            s_buf.at[me // owner_tile], stats_ref.at[me], own_sem.at[1 + held]
        )
    )
    for copy in mine:
        copy.start()
    s_all = stats_ref.at[0 : devices - 1]
    whole_wait(s_all, s_recv)
    mine[-1].wait()

    def levels(of_side):
        return jnp.concatenate(
            [
                stats_ref[of_side * half + head // held, head % held : head % held + 1, :]
                for head in range(HEADS)
            ],
            axis=0,
        )

    low, high = levels(0), levels(1)
    share = jnp.concatenate(
        [
            1.0 / (1.0 + jnp.exp(high - low)),
            1.0 / (1.0 + jnp.exp(low - high)),
            jnp.zeros((128 - 2 * HEADS, 128), jnp.float32),
        ],
        axis=0,
    )
    shares[...] = jnp.transpose(share)
    for head in range(held):
        whole_wait(q_all(head), q_send.at[head])
        for which in range(4):
            whole_wait(kv_all(head, which), kv_send.at[head, which])
    for copy in mine[:-1]:
        copy.wait()
    whole_wait(s_all, s_send)
    put_shares = pltpu.make_async_copy(
        shares.at[row_slab(me % owner_tile, tok_dev), :], shares_ref, own_sem.at[0]
    )
    put_shares.start()
    for head in range(held):
        o_all = o_buf.at[head, 0 : (devices - 1) * tok_dev, :]
        whole_wait(o_all, o_send.at[head])
        whole_wait(o_all, o_recv.at[head])
    put_shares.wait()


def merge_kernel(parts_in, shares_in, out_ref, parts, mine, merged, sems, out_sems):
    width = out_ref.shape[1]
    chunks = out_sems.shape[0]
    wide = width // chunks
    spans = [pl.ds(chunk * wide, wide) for chunk in range(chunks)]
    shares_copy = pltpu.make_async_copy(shares_in, mine, sems.at[chunks])
    shares_copy.start()
    copies = [
        pltpu.make_async_copy(parts_in.at[:, :, at], parts.at[:, :, at], sems.at[chunk])
        for chunk, at in enumerate(spans)
    ]
    for copy in copies:
        copy.start()
    shares_copy.wait()
    outs = []
    for chunk, span in enumerate(spans):
        copies[chunk].wait()
        for head in range(chunk * wide // HEAD_DIM, (chunk + 1) * wide // HEAD_DIM):
            at = slice(head * HEAD_DIM, (head + 1) * HEAD_DIM)
            low = parts[0, :, at].astype(jnp.float32) * mine[:, head : head + 1]
            high = parts[1, :, at].astype(jnp.float32) * mine[:, HEADS + head : HEADS + head + 1]
            merged[:, at] = (low + high).astype(jnp.bfloat16)
        out = pltpu.make_async_copy(merged.at[:, span], out_ref.at[:, span], out_sems.at[chunk])
        out.start()
        outs.append(out)
    for out in outs:
        out.wait()


def halves(queries, fresh_keys, fresh_values, stale_keys, stale_values, patch_starts, order_starts):
    devices = lax.axis_size("tok")
    tok_dev, width = queries.shape
    half = devices // 2
    held = HEADS // half
    tokens, keys = devices * tok_dev, half * tok_dev
    anywhere = pl.BlockSpec(memory_space=pl.ANY)
    scalars = pl.BlockSpec(memory_space=pltpu.SMEM)
    dma = pltpu.SemaphoreType.DMA
    parts, shares = pl.pallas_call(
        functools.partial(halves_kernel, devices),
        out_shape=(
            jax.ShapeDtypeStruct((2, tok_dev, width), jnp.bfloat16),
            jax.ShapeDtypeStruct((tok_dev, 128), jnp.float32),
        ),
        in_specs=[scalars] * 2 + [anywhere] * 5,
        out_specs=(anywhere, anywhere),
        scratch_shapes=[
            pltpu.VMEM((held, tokens, HEAD_DIM), jnp.bfloat16),
            pltpu.VMEM((held, 4, keys, HEAD_DIM), jnp.bfloat16),
            pltpu.VMEM((tokens, keys), jnp.bfloat16),
            pltpu.VMEM((tokens, keys), jnp.bfloat16),
            pltpu.VMEM((held, tokens, HEAD_DIM), jnp.bfloat16),
            pltpu.VMEM((tokens // 128, held, 128), jnp.float32),
            pltpu.VMEM((devices, held, 128), jnp.float32),
            pltpu.VMEM((128, 128), jnp.float32),
            pltpu.VMEM((tokens, HEAD_DIM), jnp.int32),
            pltpu.VMEM((8, keys), jnp.int32),
            dma((held,)),
            dma((held,)),
            dma((held, 4)),
            dma((held, 4)),
            dma((held,)),
            dma((2 + held,)),
            dma((held, 4)),
            dma((held,)),
            dma((held,)),
            dma,
            dma,
        ],
        compiler_params=pltpu.CompilerParams(
            collective_id=0, has_side_effects=True, vmem_limit_bytes=60 * 1024 * 1024
        ),
    )(patch_starts, order_starts, queries, fresh_keys, stale_keys, fresh_values, stale_values)
    return pl.pallas_call(
        merge_kernel,
        out_shape=jax.ShapeDtypeStruct((tok_dev, width), jnp.bfloat16),
        in_specs=[anywhere, anywhere],
        out_specs=anywhere,
        scratch_shapes=[
            pltpu.VMEM((2, tok_dev, width), jnp.bfloat16),
            pltpu.VMEM((tok_dev, 128), jnp.float32),
            pltpu.VMEM((tok_dev, width), jnp.bfloat16),
            dma((5,)),
            dma((4,)),
        ],
        compiler_params=pltpu.CompilerParams(vmem_limit_bytes=60 * 1024 * 1024),
    )(parts, shares)


def solution(mesh):
    placed = (P(("groups", "tok"), None),) * 5 + (P("groups"),) * 2
    devices = mesh.shape["tok"]

    def body(*arrays):
        tok_dev = arrays[0].shape[0]
        split = devices % 2 == 0 and HEADS % (devices // 2) == 0
        split = split and 128 % tok_dev == 0 and devices * tok_dev % 512 == 0
        return (halves if split else shards)(*arrays)

    return jax.shard_map(
        body, mesh=mesh, in_specs=placed, out_specs=P(("groups", "tok"), None), check_vma=False
    )
```

```python
import functools
import math

import jax
import jax.numpy as jnp
from jax import lax
from jax.experimental import pallas as pl
from jax.experimental.pallas import tpu as pltpu
from jax.sharding import PartitionSpec as P

HEADS = 16
HEAD_DIM = 128
MESH = pl.DeviceIdType.MESH


def attention_kernel(
    devices,
    patch_starts,
    order_starts,
    queries,
    fresh_keys,
    stale_keys,
    fresh_values,
    stale_values,
    out_ref,
    q_buf,
    kv_buf,
    p_fresh,
    p_stale,
    o_buf,
    q_rank,
    k_rank,
    send_sems,
    recv_sems,
    own_sem,
    out_send,
    out_recv,
):
    me = lax.axis_index("tok")
    tok_dev = queries.shape[0]
    group_size = devices // HEADS
    slab = tok_dev // group_size
    tokens = devices * tok_dev
    rows = devices * slab
    my_head = me // group_size
    my_member = me % group_size
    barrier = pltpu.get_barrier_semaphore()

    def peer_of(step):
        return lax.rem(me + step, devices)

    def columns(head):
        return pl.ds(pl.multiple_of(head * HEAD_DIM, HEAD_DIM), HEAD_DIM)

    def row_slab(index, size):
        return pl.ds(pl.multiple_of(index * size, size), size)

    def greet(step, carry):
        pl.semaphore_signal(barrier, inc=1, device_id={"tok": peer_of(step)}, device_id_type=MESH)
        return carry

    lax.fori_loop(1, devices, greet, 0)

    sources = (queries, fresh_keys, stale_keys, fresh_values, stale_values)

    def source_view(which, device):
        head, member = device // group_size, device % group_size
        if which == 0:
            return queries.at[row_slab(member, slab), columns(head)]
        return sources[which].at[:, columns(head)]

    def landing(which, device):
        if which == 0:
            return q_buf.at[row_slab(device, slab), :]
        return kv_buf.at[which - 1, row_slab(device, tok_dev), :]

    own = [
        pltpu.make_async_copy(source_view(which, me), landing(which, me), own_sem.at[which])
        for which in range(5)
    ]
    for copy in own:
        copy.start()
    pl.semaphore_wait(barrier, devices - 1)

    for which in range(5):

        def send(step, carry, which=which):
            peer = peer_of(step)
            pltpu.make_async_remote_copy(
                src_ref=source_view(which, peer),
                dst_ref=landing(which, me),
                send_sem=send_sems.at[which],
                recv_sem=recv_sems.at[which],
                device_id={"tok": peer},
                device_id_type=MESH,
            ).start()
            return carry

        lax.fori_loop(1, devices, send, 0)

    patches = patch_starts.shape[0]
    starts = [patch_starts[p] for p in range(patches)]
    orders = [order_starts[p] for p in range(patches)]
    ranks = []
    for p in range(patches):
        rank = jnp.int32(0)
        for i in range(patches):
            rank = rank + jnp.where(orders[i] == starts[p], jnp.int32(i), jnp.int32(0))
        ranks.append(rank)
    jumps = [ranks[0]] + [ranks[p] - ranks[p - 1] for p in range(1, patches)]

    def rank_at(positions):
        total = jnp.zeros(positions.shape, jnp.int32)
        for p in range(patches):
            total = total + jnp.where(positions >= starts[p], jumps[p], 0)
        return total

    k_rank[...] = rank_at(lax.broadcasted_iota(jnp.int32, k_rank.shape, 1))

    def fill_rank(device, carry):
        base = device * tok_dev + my_member * slab
        q_rank[row_slab(device, slab), :] = rank_at(
            base + lax.broadcasted_iota(jnp.int32, (slab, HEAD_DIM), 0)
        )
        return carry

    lax.fori_loop(0, devices, fill_rank, 0)

    def all_of(which):
        size = (devices - 1) * (slab if which == 0 else tok_dev)
        return q_buf.at[0:size, :] if which == 0 else kv_buf.at[which - 1, 0:size, :]

    def arrived(which):
        view = all_of(which)
        pltpu.make_async_copy(view, view, recv_sems.at[which]).wait()
        own[which].wait()

    for which in range(3):
        arrived(which)

    score_scale = 1.0 / math.sqrt(HEAD_DIM)
    block = max(slab, min(rows, (1 << 18) // tokens))
    blocks = rows // block
    dims = (((1,), (1,)), ((), ()))

    def probs_block(i, carry):
        at = row_slab(i, block)
        q = q_buf[at, :]
        fresh = lax.dot_general(q, kv_buf[0], dims, preferred_element_type=jnp.float32)
        stale = lax.dot_general(q, kv_buf[1], dims, preferred_element_type=jnp.float32)
        fresh_ok = k_rank[0:1, :] <= q_rank[at, 0:1]
        scores = jnp.where(fresh_ok, fresh, stale) * score_scale
        top = jnp.max(scores, axis=1, keepdims=True)
        weights = jnp.exp(scores - top)
        total = jnp.sum(weights, axis=1, keepdims=True)
        probs = weights * (1.0 / total)
        p_fresh[at, :] = jnp.where(fresh_ok, probs, 0.0).astype(jnp.bfloat16)
        p_stale[at, :] = jnp.where(fresh_ok, 0.0, probs).astype(jnp.bfloat16)
        return carry

    lax.fori_loop(0, blocks, probs_block, 0)

    for which in range(3, 5):
        arrived(which)

    per_block = block // slab

    def give_back(i):
        def one(j, carry):
            target = i * per_block + j

            @pl.when(target != me)
            def _():
                pltpu.make_async_remote_copy(
                    src_ref=o_buf.at[row_slab(target, slab), :],
                    dst_ref=out_ref.at[row_slab(my_member, slab), columns(my_head)],
                    send_sem=out_send,
                    recv_sem=out_recv,
                    device_id={"tok": target},
                    device_id_type=MESH,
                ).start()

            return carry

        lax.fori_loop(0, per_block, one, 0)

    def attend_block(i, carry):
        at = row_slab(i, block)
        mixed = jnp.dot(p_fresh[at, :], kv_buf[2], preferred_element_type=jnp.float32)
        mixed = mixed + jnp.dot(p_stale[at, :], kv_buf[3], preferred_element_type=jnp.float32)
        o_buf[at, :] = mixed.astype(jnp.bfloat16)
        give_back(i)
        return carry

    lax.fori_loop(0, blocks, attend_block, 0)
    mine = pltpu.make_async_copy(
        o_buf.at[row_slab(me, slab), :],
        out_ref.at[row_slab(my_member, slab), columns(my_head)],
        own_sem.at[0],
    )
    mine.start()
    for which in range(5):
        view = all_of(which)
        pltpu.make_async_copy(view, view, send_sems.at[which]).wait()
    view = o_buf.at[0 : (devices - 1) * slab, :]
    mine.wait()
    pltpu.make_async_copy(view, view, out_send).wait()
    pltpu.make_async_copy(view, view, out_recv).wait()


def shards(queries, fresh_keys, fresh_values, stale_keys, stale_values, patch_starts, order_starts):
    devices = lax.axis_size("tok")
    tok_dev, width = queries.shape
    slab = tok_dev // (devices // HEADS)
    tokens, rows = devices * tok_dev, devices * slab
    anywhere = pl.BlockSpec(memory_space=pl.ANY)
    scalars = pl.BlockSpec(memory_space=pltpu.SMEM)
    return pl.pallas_call(
        functools.partial(attention_kernel, devices),
        out_shape=jax.ShapeDtypeStruct((tok_dev, width), jnp.bfloat16),
        in_specs=[scalars] * 2 + [anywhere] * 5,
        out_specs=anywhere,
        scratch_shapes=[
            pltpu.VMEM((rows, HEAD_DIM), jnp.bfloat16),
            pltpu.VMEM((4, tokens, HEAD_DIM), jnp.bfloat16),
            pltpu.VMEM((rows, tokens), jnp.bfloat16),
            pltpu.VMEM((rows, tokens), jnp.bfloat16),
            pltpu.VMEM((rows, HEAD_DIM), jnp.bfloat16),
            pltpu.VMEM((rows, HEAD_DIM), jnp.int32),
            pltpu.VMEM((8, tokens), jnp.int32),
            pltpu.SemaphoreType.DMA((5,)),
            pltpu.SemaphoreType.DMA((5,)),
            pltpu.SemaphoreType.DMA((5,)),
            pltpu.SemaphoreType.DMA,
            pltpu.SemaphoreType.DMA,
        ],
        compiler_params=pltpu.CompilerParams(
            collective_id=0, has_side_effects=True, vmem_limit_bytes=60 * 1024 * 1024
        ),
    )(
        patch_starts,
        order_starts,
        queries,
        fresh_keys,
        stale_keys,
        fresh_values,
        stale_values,
    )


def rank_table(patch_starts, order_starts):
    patches = patch_starts.shape[0]
    starts = [patch_starts[p] for p in range(patches)]
    orders = [order_starts[p] for p in range(patches)]
    ranks = []
    for p in range(patches):
        rank = jnp.int32(0)
        for i in range(patches):
            rank = rank + jnp.where(orders[i] == starts[p], jnp.int32(i), jnp.int32(0))
        ranks.append(rank)
    jumps = [ranks[0]] + [ranks[p] - ranks[p - 1] for p in range(1, patches)]

    def rank_at(positions):
        total = jnp.zeros(positions.shape, jnp.int32)
        for p in range(patches):
            total = total + jnp.where(positions >= starts[p], jumps[p], 0)
        return total

    return rank_at


def halves_kernel(
    devices,
    patch_starts,
    order_starts,
    queries,
    fresh_keys,
    stale_keys,
    fresh_values,
    stale_values,
    parts_ref,
    shares_ref,
    q_buf,
    kv_buf,
    p_fresh,
    p_stale,
    o_buf,
    s_buf,
    stats_ref,
    shares,
    q_rank,
    k_rank,
    q_send,
    q_recv,
    kv_send,
    kv_recv,
    own_q_sem,
    own_sem,
    own_kv_sem,
    o_send,
    o_recv,
    s_send,
    s_recv,
):
    me = lax.axis_index("tok")
    tok_dev = queries.shape[0]
    half = devices // 2
    held = HEADS // half
    tokens = devices * tok_dev
    keys = half * tok_dev
    side, place = me // half, me % half
    barrier = pltpu.get_barrier_semaphore()

    def peer_of(step):
        return lax.rem(me + step, devices)

    def near_peer(step):
        return side * half + lax.rem(place + step, half)

    def columns(head):
        return pl.ds(pl.multiple_of(head * HEAD_DIM, HEAD_DIM), HEAD_DIM)

    def row_slab(index, size):
        return pl.ds(pl.multiple_of(index * size, size), size)

    def greet(step, carry):
        pl.semaphore_signal(barrier, inc=1, device_id={"tok": peer_of(step)}, device_id_type=MESH)
        return carry

    lax.fori_loop(1, devices, greet, 0)

    sources = (fresh_keys, stale_keys, fresh_values, stale_values)

    def q_source(head, device):
        return queries.at[:, columns(device % half * held + head)]

    def kv_source(head, which, device):
        return sources[which].at[:, columns(device % half * held + head)]

    def q_landing(head, device):
        return q_buf.at[head, row_slab(device, tok_dev), :]

    def kv_landing(head, which, device):
        return kv_buf.at[head, which, row_slab(device % half, tok_dev), :]

    own_q = [
        pltpu.make_async_copy(q_source(head, me), q_landing(head, me), own_q_sem.at[head])
        for head in range(held)
    ]
    for copy in own_q:
        copy.start()
    own_kv = [
        [
            pltpu.make_async_copy(
                kv_source(head, which, me), kv_landing(head, which, me), own_kv_sem.at[head, which]
            )
            for which in range(4)
        ]
        for head in range(held)
    ]
    for group in own_kv:
        for copy in group:
            copy.start()
    pl.semaphore_wait(barrier, devices - 1)

    for head in range(held):

        def send_q(step, carry, head=head):
            peer = peer_of(step)
            pltpu.make_async_remote_copy(
                src_ref=q_source(head, peer),
                dst_ref=q_landing(head, me),
                send_sem=q_send.at[head],
                recv_sem=q_recv.at[head],
                device_id={"tok": peer},
                device_id_type=MESH,
            ).start()
            return carry

        lax.fori_loop(1, devices, send_q, 0)
        for which in range(4):

            def send_kv(step, carry, head=head, which=which):
                peer = near_peer(step)
                pltpu.make_async_remote_copy(
                    src_ref=kv_source(head, which, peer),
                    dst_ref=kv_landing(head, which, me),
                    send_sem=kv_send.at[head, which],
                    recv_sem=kv_recv.at[head, which],
                    device_id={"tok": peer},
                    device_id_type=MESH,
                ).start()
                return carry

            lax.fori_loop(1, half, send_kv, 0)

    rank_at = rank_table(patch_starts, order_starts)
    k_rank[...] = rank_at(keys * side + lax.broadcasted_iota(jnp.int32, k_rank.shape, 1))

    def fill_rank(device, carry):
        q_rank[row_slab(device, tok_dev), :] = rank_at(
            device * tok_dev + lax.broadcasted_iota(jnp.int32, (tok_dev, HEAD_DIM), 0)
        )
        return carry

    lax.fori_loop(0, devices, fill_rank, 0)

    def whole_wait(view, sem):
        pltpu.make_async_copy(view, view, sem).wait()

    def q_all(head):
        return q_buf.at[head, 0 : (devices - 1) * tok_dev, :]

    def kv_all(head, which):
        return kv_buf.at[head, which, 0 : (half - 1) * tok_dev, :]

    def arrived(head, which):
        whole_wait(kv_all(head, which), kv_recv.at[head, which])
        own_kv[head][which].wait()

    score_scale = 1.0 / math.sqrt(HEAD_DIM)
    block = min(tokens, 512)
    blocks = tokens // block
    per_block = block // tok_dev
    dims = (((1,), (1,)), ((), ()))
    owner_tile = 128 // tok_dev

    for head in range(held):
        whole_wait(q_all(head), q_recv.at[head])
        own_q[head].wait()
        arrived(head, 0)
        arrived(head, 1)

        def probs_block(i, carry, head=head):
            at = row_slab(i, block)
            q = q_buf[head, at, :]
            fresh = lax.dot_general(q, kv_buf[head, 0], dims, preferred_element_type=jnp.float32)
            stale = lax.dot_general(q, kv_buf[head, 1], dims, preferred_element_type=jnp.float32)
            fresh_ok = k_rank[0:1, :] <= q_rank[at, 0:1]
            scores = jnp.where(fresh_ok, fresh, stale) * score_scale
            top = jnp.max(scores, axis=1, keepdims=True)
            weights = jnp.exp(scores - top)
            total = jnp.sum(weights, axis=1, keepdims=True)
            probs = weights * (1.0 / total)
            p_fresh[at, :] = jnp.where(fresh_ok, probs, 0.0).astype(jnp.bfloat16)
            p_stale[at, :] = jnp.where(fresh_ok, 0.0, probs).astype(jnp.bfloat16)
            level = jnp.broadcast_to(top + jnp.log(total), (block, 128))
            for tile in range(block // 128):
                turned = jnp.transpose(level[tile * 128 : (tile + 1) * 128, :])
                s_buf[i * (block // 128) + tile, head : head + 1, :] = turned[0:1, :]
            return carry

        lax.fori_loop(0, blocks, probs_block, 0)
        arrived(head, 2)
        arrived(head, 3)

        if head == held - 1:

            def send_stats(step, carry):
                peer = peer_of(step)
                pltpu.make_async_remote_copy(
                    src_ref=s_buf.at[peer // owner_tile],
                    dst_ref=stats_ref.at[me],
                    send_sem=s_send,
                    recv_sem=s_recv,
                    device_id={"tok": peer},
                    device_id_type=MESH,
                ).start()
                return carry

        def attend_block(i, carry, head=head):
            at = row_slab(i, block)
            mixed = jnp.dot(p_fresh[at, :], kv_buf[head, 2], preferred_element_type=jnp.float32)
            mixed = mixed + jnp.dot(
                p_stale[at, :], kv_buf[head, 3], preferred_element_type=jnp.float32
            )
            o_buf[head, at, :] = mixed.astype(jnp.bfloat16)

            def give_back(j, carry):
                target = i * per_block + j

                @pl.when(target != me)
                def _():
                    pltpu.make_async_remote_copy(
                        src_ref=o_buf.at[head, row_slab(target, tok_dev), :],
                        dst_ref=parts_ref.at[side, :, columns(place * held + head)],
                        send_sem=o_send.at[head],
                        recv_sem=o_recv.at[head],
                        device_id={"tok": target},
                        device_id_type=MESH,
                    ).start()

                return carry

            lax.fori_loop(0, per_block, give_back, 0)
            return carry

        if head == held - 1:
            lax.fori_loop(1, devices, send_stats, 0)
        lax.fori_loop(0, blocks, attend_block, 0)

    mine = [
        pltpu.make_async_copy(
            o_buf.at[head, row_slab(me, tok_dev), :],
            parts_ref.at[side, :, columns(place * held + head)],
            own_sem.at[1 + head],
        )
        for head in range(held)
    ]
    mine.append(
        pltpu.make_async_copy(
            s_buf.at[me // owner_tile], stats_ref.at[me], own_sem.at[1 + held]
        )
    )
    for copy in mine:
        copy.start()
    s_all = stats_ref.at[0 : devices - 1]
    whole_wait(s_all, s_recv)
    mine[-1].wait()

    def levels(of_side):
        return jnp.concatenate(
            [
                stats_ref[of_side * half + head // held, head % held : head % held + 1, :]
                for head in range(HEADS)
            ],
            axis=0,
        )

    low, high = levels(0), levels(1)
    share = jnp.concatenate(
        [
            1.0 / (1.0 + jnp.exp(high - low)),
            1.0 / (1.0 + jnp.exp(low - high)),
            jnp.zeros((128 - 2 * HEADS, 128), jnp.float32),
        ],
        axis=0,
    )
    shares[...] = jnp.transpose(share)
    for head in range(held):
        whole_wait(q_all(head), q_send.at[head])
        for which in range(4):
            whole_wait(kv_all(head, which), kv_send.at[head, which])
    for copy in mine[:-1]:
        copy.wait()
    whole_wait(s_all, s_send)
    put_shares = pltpu.make_async_copy(
        shares.at[row_slab(me % owner_tile, tok_dev), :], shares_ref, own_sem.at[0]
    )
    put_shares.start()
    for head in range(held):
        o_all = o_buf.at[head, 0 : (devices - 1) * tok_dev, :]
        whole_wait(o_all, o_send.at[head])
        whole_wait(o_all, o_recv.at[head])
    put_shares.wait()


def merge_kernel(parts_in, shares_in, out_ref, parts, mine, merged, sems, out_sems):
    width = out_ref.shape[1]
    chunks = out_sems.shape[0]
    wide = width // chunks
    spans = [pl.ds(chunk * wide, wide) for chunk in range(chunks)]
    shares_copy = pltpu.make_async_copy(shares_in, mine, sems.at[chunks])
    shares_copy.start()
    copies = [
        pltpu.make_async_copy(parts_in.at[:, :, at], parts.at[:, :, at], sems.at[chunk])
        for chunk, at in enumerate(spans)
    ]
    for copy in copies:
        copy.start()
    shares_copy.wait()
    outs = []
    for chunk, span in enumerate(spans):
        copies[chunk].wait()
        for head in range(chunk * wide // HEAD_DIM, (chunk + 1) * wide // HEAD_DIM):
            at = slice(head * HEAD_DIM, (head + 1) * HEAD_DIM)
            low = parts[0, :, at].astype(jnp.float32) * mine[:, head : head + 1]
            high = parts[1, :, at].astype(jnp.float32) * mine[:, HEADS + head : HEADS + head + 1]
            merged[:, at] = (low + high).astype(jnp.bfloat16)
        out = pltpu.make_async_copy(merged.at[:, span], out_ref.at[:, span], out_sems.at[chunk])
        out.start()
        outs.append(out)
    for out in outs:
        out.wait()


def halves(queries, fresh_keys, fresh_values, stale_keys, stale_values, patch_starts, order_starts):
    devices = lax.axis_size("tok")
    tok_dev, width = queries.shape
    half = devices // 2
    held = HEADS // half
    tokens, keys = devices * tok_dev, half * tok_dev
    anywhere = pl.BlockSpec(memory_space=pl.ANY)
    scalars = pl.BlockSpec(memory_space=pltpu.SMEM)
    dma = pltpu.SemaphoreType.DMA
    parts, shares = pl.pallas_call(
        functools.partial(halves_kernel, devices),
        out_shape=(
            jax.ShapeDtypeStruct((2, tok_dev, width), jnp.bfloat16),
            jax.ShapeDtypeStruct((tok_dev, 128), jnp.float32),
        ),
        in_specs=[scalars] * 2 + [anywhere] * 5,
        out_specs=(anywhere, anywhere),
        scratch_shapes=[
            pltpu.VMEM((held, tokens, HEAD_DIM), jnp.bfloat16),
            pltpu.VMEM((held, 4, keys, HEAD_DIM), jnp.bfloat16),
            pltpu.VMEM((tokens, keys), jnp.bfloat16),
            pltpu.VMEM((tokens, keys), jnp.bfloat16),
            pltpu.VMEM((held, tokens, HEAD_DIM), jnp.bfloat16),
            pltpu.VMEM((tokens // 128, held, 128), jnp.float32),
            pltpu.VMEM((devices, held, 128), jnp.float32),
            pltpu.VMEM((128, 128), jnp.float32),
            pltpu.VMEM((tokens, HEAD_DIM), jnp.int32),
            pltpu.VMEM((8, keys), jnp.int32),
            dma((held,)),
            dma((held,)),
            dma((held, 4)),
            dma((held, 4)),
            dma((held,)),
            dma((2 + held,)),
            dma((held, 4)),
            dma((held,)),
            dma((held,)),
            dma,
            dma,
        ],
        compiler_params=pltpu.CompilerParams(
            collective_id=0, has_side_effects=True, vmem_limit_bytes=60 * 1024 * 1024
        ),
    )(patch_starts, order_starts, queries, fresh_keys, stale_keys, fresh_values, stale_values)
    return pl.pallas_call(
        merge_kernel,
        out_shape=jax.ShapeDtypeStruct((tok_dev, width), jnp.bfloat16),
        in_specs=[anywhere, anywhere],
        out_specs=anywhere,
        scratch_shapes=[
            pltpu.VMEM((2, tok_dev, width), jnp.bfloat16),
            pltpu.VMEM((tok_dev, 128), jnp.float32),
            pltpu.VMEM((tok_dev, width), jnp.bfloat16),
            dma((3,)),
            dma((2,)),
        ],
        compiler_params=pltpu.CompilerParams(vmem_limit_bytes=60 * 1024 * 1024),
    )(parts, shares)


def solution(mesh):
    placed = (P(("groups", "tok"), None),) * 5 + (P("groups"),) * 2
    devices = mesh.shape["tok"]

    def body(*arrays):
        tok_dev = arrays[0].shape[0]
        split = devices % 2 == 0 and HEADS % (devices // 2) == 0
        split = split and 128 % tok_dev == 0 and devices * tok_dev % 512 == 0
        return (halves if split else shards)(*arrays)

    return jax.shard_map(
        body, mesh=mesh, in_specs=placed, out_specs=P(("groups", "tok"), None), check_vma=False
    )
```
